32 devices in a mesh: dp: 4 (over z), seq: 8 (over y, x, core).
Axes of the slice: x: 2, y: 2, z: 4, core: 2. Of those that a mesh axis runs over, the one named last changes fastest.
Arguments:
- slide_tiles: bfloat16 [64, 256, 384], P(('dp', 'seq')), parts along dimension 0, may hold values from -6 to 6
- norm_gain: float32 [2, 384], replicated, may hold values from 0.1 to 1.9
- in_weight: bfloat16 [2, 384, 1536], replicated, may hold values from -0.3125 to 0.3125
- state_weight: bfloat16 [2, 384, 44], replicated, may hold values from -0.3125 to 0.3125
- conv_weight: float32 [2, 4, 800], replicated, may hold values from -2.5 to 2.5
- conv_bias: float32 [2, 800], replicated, may hold values from -0.5 to 0.5
- step_bias: float32 [2, 12], replicated, may hold values from -5 to -3
- decay_log: float32 [2, 12], replicated, may hold values from -8.5 to 1
- skip_gain: float32 [2, 12], replicated, may hold values from 0.5 to 1.5
- out_gain: float32 [2, 768], replicated, may hold values from 0.1 to 1.9
- out_weight: bfloat16 [2, 768, 384], replicated, may hold values from -0.21875 to 0.21875
Outputs:
- tile_out: bfloat16 [64, 256, 384], P(('dp', 'seq')), parts along dimension 0
The draws below stay inside these ranges and needn't reach their ends.
There are 4 independent parts, one for each index of `dp`. The reference program is written for one: setup_inputs(seed, part) draws one part's arguments, and reference() takes and returns one part's arrays. A program takes and returns all parts, laid end to end along the dimension named above; an argument that names none is the same for every part. Nothing has to cross between parts.
All inputs are finite; a program needn't handle non-finite values.
Results may differ from the reference program's by a relative error of at most 0.014.
Values may be sent and summed in bfloat16 or wider, within the bound.
A program may use at most 64 MiB of HBM per device.

```python
import jax
import jax.numpy as jnp
from jax import lax

D = 384
HEADS = 12
HEADDIM = 64
STATE = 16
KERNEL = 4
GROUP = 256
COLS = 256
INNER = 768
ROWS = 16


def draw_decay_log(key, part):
    values = jax.random.uniform(key, (2, HEADS), jnp.float32, -8.5, 1.0)
    return values


def shard_levels(key, dims, cuts, least, top_value):
    loudness = 1.0
    for dim, parts in cuts:
        draws = jax.random.uniform(jax.random.fold_in(jax.random.fold_in(key, 6), dim), (parts,), jnp.float32, least / len(cuts), top_value / len(cuts))
        loudness = loudness * jnp.repeat(jnp.exp(draws), dims[dim] // parts).reshape((-1,) + (1,) * (len(dims) - 1 - dim))
    return loudness


def scatter_about(own_key, dims, deviation, most, shards=(), kind=jnp.bfloat16):
    entries = jax.random.normal(own_key, dims, jnp.float32) * deviation
    if len(shards) > 0:
        entries = shard_levels(own_key, dims, shards, -0.22, 0.18) * entries
    return jnp.clip(entries, min=-most, max=most).astype(kind)


def setup_inputs(seed: int = 0, part: int = 0) -> dict:
    streams_of = jax.random.split(jax.random.key(seed), 12)
    part_splits = jax.random.split(jax.random.fold_in(streams_of[11], part), 12)
    return {
        "slide_tiles": scatter_about(part_splits[0], (ROWS, COLS, D), 1.0, 6.0, ((0, 8),)),
        "norm_gain": jnp.clip(1.0 + 0.18 * jax.random.normal(streams_of[1], (2, D), jnp.float32), 0.1, 1.9),
        "in_weight": scatter_about(streams_of[2], (2, D, 2 * INNER), D ** -0.5, 0.3125),
        "state_weight": scatter_about(streams_of[3], (2, D, 2 * STATE + HEADS), D ** -0.5, 0.3125),
        "conv_weight": scatter_about(streams_of[4], (2, KERNEL, INNER + 2 * STATE), 0.5, 2.5, (), jnp.float32),
        "conv_bias": jnp.clip(jax.random.uniform(streams_of[5], (2, INNER + 2 * STATE), jnp.float32, -0.5, 0.5), -0.5, 0.5),
        "step_bias": jnp.clip(jax.random.uniform(streams_of[6], (2, HEADS), jnp.float32, -5.0, -3.0), -5.0, -3.0),
        "decay_log": draw_decay_log(jax.random.fold_in(streams_of[11], 71), part),
        "skip_gain": jnp.clip(jax.random.uniform(streams_of[8], (2, HEADS), jnp.float32, 0.5, 1.5), 0.5, 1.5),
        "out_gain": jnp.clip(1.0 + 0.18 * jax.random.normal(streams_of[9], (2, INNER), jnp.float32), 0.1, 1.9),
        "out_weight": scatter_about(streams_of[10], (2, INNER, D), INNER ** -0.5, 0.21875),
    }


epsilon = 1e-05

def rms_scaled(values, scale_gain):
    values = values.astype(jnp.float32)
    return values * lax.rsqrt(lax.optimization_barrier(jnp.mean(values * values, axis=-1, keepdims=True)) + epsilon) * scale_gain

def group_update(carry_state, group_in):
    group_x, group_b, group_c, group_step, group_rate = group_in
    cumulative = jnp.cumsum(group_rate, axis=0)
    positions = jnp.arange(group_x.shape[0])
    lower_mask = positions[:, None] >= positions[None, :]
    cum_heads = cumulative.T
    differences = cum_heads[:, :, None] - cum_heads[:, None, :]
    decay_mask = jnp.exp(jnp.where(lower_mask[None], differences, -jnp.inf))
    scores = jnp.dot(group_c, group_b.T, preferred_element_type=jnp.float32)
    weights = (scores[None] * decay_mask * group_step.T[:, None, :]).astype(jnp.bfloat16)
    intra_out = jnp.einsum('hts,shp->thp', weights.astype(jnp.float32), group_x.astype(jnp.float32))
    inter_out = jnp.exp(cumulative)[:, :, None] * jnp.einsum('tn,hpn->thp', group_c.astype(jnp.float32), carry_state, precision=lax.Precision.HIGHEST)
    tail_weight = jnp.exp(cumulative[-1][None, :] - cumulative) * group_step
    weighted_x = (group_x.astype(jnp.float32) * tail_weight[:, :, None]).astype(jnp.bfloat16)
    local_state = jnp.einsum('shp,sn->hpn', weighted_x.astype(jnp.float32), group_b.astype(jnp.float32))
    next_state = jnp.exp(cumulative[-1])[:, None, None] * carry_state + local_state
    return (next_state, intra_out + inter_out)

def mixer(sequence, layer, norm_gain, in_weight, state_weight, conv_weight, conv_bias, step_bias, decay_log, skip_gain, out_gain):
    length = sequence.shape[0]
    inner_width = in_weight.shape[2] // 2
    normed = rms_scaled(sequence, norm_gain[layer]).astype(jnp.bfloat16)
    gate_x = jnp.dot(normed, in_weight[layer], preferred_element_type=jnp.float32).astype(jnp.bfloat16)
    state_proj = jnp.dot(normed, state_weight[layer], preferred_element_type=jnp.float32).astype(jnp.bfloat16)
    conv_in = jnp.concatenate([gate_x[:, inner_width:], state_proj[:, :2 * STATE]], axis=1)
    margin = conv_weight.shape[1] - 1
    padded = jnp.concatenate([jnp.zeros((margin, conv_in.shape[1]), jnp.bfloat16), conv_in], axis=0)
    conv_sum = jnp.zeros((length, conv_in.shape[1]), jnp.float32) + conv_bias[layer][None, :]
    for offset in range(margin + 1):
        conv_sum = conv_sum + conv_weight[layer, offset][None, :] * padded[offset:offset + length].astype(jnp.float32)
    conv_out = jax.nn.silu(conv_sum).astype(jnp.bfloat16)
    x_conv = conv_out[:, :inner_width]
    b_conv = conv_out[:, inner_width:inner_width + STATE]
    c_conv = conv_out[:, inner_width + STATE:]
    step_size = jax.nn.softplus(state_proj[:, 2 * STATE:].astype(jnp.float32) + step_bias[layer][None, :])
    log_rates = -step_size * jnp.exp(decay_log[layer])[None, :]
    group_count = length // GROUP
    inputs = (x_conv.reshape(group_count, GROUP, HEADS, HEADDIM), b_conv.reshape(group_count, GROUP, STATE), c_conv.reshape(group_count, GROUP, STATE), step_size.reshape(group_count, GROUP, HEADS), log_rates.reshape(group_count, GROUP, HEADS))
    final_state, outputs = lax.scan(group_update, jnp.zeros((HEADS, HEADDIM, STATE), jnp.float32), inputs)
    y_total = outputs.reshape(length, HEADS, HEADDIM)
    y_total = y_total + skip_gain[layer][None, :, None] * x_conv.reshape(length, HEADS, HEADDIM).astype(jnp.float32)
    gated = y_total.reshape(length, inner_width) * jax.nn.silu(gate_x[:, :inner_width].astype(jnp.float32))
    return rms_scaled(gated, out_gain[layer]).astype(jnp.bfloat16)

def reference(slide_tiles, norm_gain, in_weight, state_weight, conv_weight, conv_bias, step_bias, decay_log, skip_gain, out_gain, out_weight):
    row_count, col_count, feature_count = slide_tiles.shape
    params = (norm_gain, in_weight, state_weight, conv_weight, conv_bias, step_bias, decay_log, skip_gain, out_gain)
    first_order = jnp.transpose(slide_tiles, (1, 0, 2)).reshape(row_count * col_count, feature_count)[::-1]
    mixed_out = mixer(first_order, 0, *params)
    after_first = (first_order.astype(jnp.float32) + jnp.dot(mixed_out, out_weight[0], preferred_element_type=jnp.float32)).astype(jnp.bfloat16)
    row_grid = jnp.transpose(after_first[::-1].reshape(col_count, row_count, feature_count), (1, 0, 2))
    second = row_grid.reshape(row_count * col_count, feature_count)
    mixed_out = mixer(second, 1, *params)
    result = (second.astype(jnp.float32) + jnp.dot(mixed_out, out_weight[1], preferred_element_type=jnp.float32)).astype(jnp.bfloat16)
    return result.reshape(row_count, col_count, feature_count)
```

```python
import functools
import math

import jax
import jax.numpy as jnp
from jax import lax
from jax.experimental import pallas as pl
from jax.experimental.pallas import tpu as pltpu
from jax.sharding import PartitionSpec as P

HEADS = 12
HEADDIM = 64
STATE = 16
LANES = 128
SUB = 8
EDGE = 16
EPS = 1e-05
LOG2E = math.log2(math.e)
MESH = pl.DeviceIdType.MESH
F32 = jnp.float32
BF16 = jnp.bfloat16


def silu(v):
    half = 0.5 * v
    return half + half * jnp.tanh(half)


def rms(v, gain):
    return v * lax.rsqrt(jnp.mean(v * v, axis=-1, keepdims=True) + EPS) * gain


def iota(shape, dim):
    return lax.broadcasted_iota(jnp.int32, shape, dim)


def dot(a, b):
    return jnp.dot(a, b, preferred_element_type=F32)


def dot_nt(a, b):
    return lax.dot_general(a, b, (((1,), (1,)), ((), ())), preferred_element_type=F32)


def xor(a, b, bits):
    total = 0
    for i in range(bits):
        total = total + lax.rem(a // 2**i + b // 2**i, 2) * 2**i
    return total


def kernel(n, names, *all_refs):
    r = dict(zip(names, all_refs))
    out = r["out"]
    slide, in_hbm, out_hbm = r["slide"], r["in_hbm"], r["out_hbm"]
    me = lax.axis_index("seq")
    rows, cols, width = slide.shape
    full = rows * n
    block = cols // n
    tokens = rows * cols
    inner = in_hbm.shape[2] // 2
    taps = r["conv_weight_hbm"].shape[1]
    proj = r["state_weight_hbm"].shape[0]
    bits = n.bit_length() - 1
    chips = n // 2
    chip = me // 2
    sources = -(-(taps - 1) // rows)
    pieces = width // LANES
    edge = min(EDGE, block)
    ocols = min(16, block)
    chunks = block // ocols
    size0 = full * SUB
    size1 = min(LANES, cols)

    def remote(src, dst, send_sem, recv_sem, to):
        return pltpu.make_async_remote_copy(
            src_ref=src,
            dst_ref=dst,
            send_sem=send_sem,
            recv_sem=recv_sem,
            device_id={"seq": to},
            device_id_type=MESH,
        )

    barrier = pltpu.get_barrier_semaphore()
    for k in range(1, n):
        pl.semaphore_signal(
            barrier, inc=1, device_id={"seq": lax.rem(me + k, n)}, device_id_type=MESH
        )

    w_sem = r["w_sem"]
    local_in = [pltpu.make_async_copy(slide, r["slide_v"], w_sem.at[0])]
    small_names = [name[:-4] for name in names if name.endswith("_hbm") and name[:-4] in names]
    small_names = [name for name in small_names if name not in ("in", "out")]
    smalls = [
        pltpu.make_async_copy(r[name + "_hbm"], r[name], w_sem.at[1 + i])
        for i, name in enumerate(small_names)
    ]
    base = 1 + len(small_names)
    weights = [
        pltpu.make_async_copy(in_hbm.at[0], r["in_w"].at[0], w_sem.at[base]),
        pltpu.make_async_copy(in_hbm.at[1], r["in_w"].at[1], w_sem.at[base + 1]),
        pltpu.make_async_copy(out_hbm, r["out_w"], w_sem.at[base + 2]),
    ]
    local_in[0].start()
    for copy in smalls:
        copy.start()
    weights[0].start()
    weights[2].start()
    weights[1].start()

    norm_gain, conv_weight, conv_bias = r["norm_gain"], r["conv_weight"], r["conv_bias"]
    in_w, out_w, out_gain = r["in_w"], r["out_w"], r["out_gain"]
    slide_v, r1, r2, o1 = r["slide_v"], r["r1"], r["r2"], r["o1"]
    edge1, edge2, pack = r["edge1"], r["edge2"], r["pack"]

    def at_cols(j):
        return pl.ds(pl.multiple_of(j * block, block), block)

    def at_rows(j):
        return pl.ds(j * rows, rows)

    local_in[0].wait()
    packf = r["packf"]
    packf[...] = jnp.zeros_like(packf)
    for j in range(n - 1):
        for i in range(rows):
            at = (j + 1) * block
            line = slide_v[i, at : at + SUB, :].astype(F32)
            for q in range(pieces):
                packf[j, i * pieces + q : i * pieces + q + 1, :] = line[
                    0:1, q * LANES : (q + 1) * LANES
                ]
    pack[...] = packf[...].astype(BF16)

    pl.semaphore_wait(barrier, n - 1)

    def first_copy(mask):
        to = xor(me, mask, bits)
        return remote(
            slide_v.at[:, at_cols(to), :],
            r1.at[at_rows(me)],
            r["s1"].at[mask],
            r["v1"].at[mask],
            to,
        )

    for mask in [1] + list(range(n - 1, 1, -1)):
        first_copy(mask).start()

    def edge1_copy(source, j):
        return remote(
            pack.at[j],
            edge1.at[source],
            r["e1s"].at[j],
            r["e1r"].at[source],
            j,
        )

    for source in range(sources):

        @pl.when(me == source)
        def _():
            for j in range(n - 1):
                if j != source:
                    edge1_copy(source, j).start()
            edge1[source] = pack[source]

    own = pltpu.make_async_copy(slide_v.at[:, at_cols(me), :], r1.at[at_rows(me)], r["l_sem"].at[0])
    own.start()

    @pl.when(me == n - 1)
    def _():
        edge1[...] = jnp.zeros_like(edge1)

    @pl.when(me == 0)
    def _():
        edge2[...] = jnp.zeros_like(edge2)

    head_mask = iota((STATE, inner), 0) == iota((STATE, inner), 1) // HEADDIM

    def spread(column):
        return jnp.sum(jnp.where(head_mask, column, 0.0), axis=0, keepdims=True)

    diag = r["diag"]
    diag[...] = jnp.where(
        iota((HEADS * STATE, inner), 0) // STATE == iota((HEADS * STATE, inner), 1) // HEADDIM,
        1.0,
        0.0,
    ).astype(BF16)

    def key0(v):
        return lax.rem(v, SUB) * full + v // SUB

    order0 = key0(iota((size0, size0), 0)), key0(iota((size0, size0), 1))
    order1 = iota((size1, size1), 0), iota((size1, size1), 1)
    r["neg0"][...] = jnp.where(order0[1] >= order0[0], 0.0, -jnp.inf)
    r["sum0"][...] = jnp.where(order0[0] >= order0[1], 1.0, 0.0).astype(BF16)
    r["neg1"][...] = jnp.where(order1[1] <= order1[0], 0.0, -jnp.inf)
    r["sum1"][...] = jnp.where(order1[0] <= order1[1], 1.0, 0.0).astype(BF16)

    small = r["small"]
    small[...] = jnp.zeros_like(small)
    p0, p1 = r["p0"], r["p1"]
    p0[...] = jnp.zeros_like(p0)
    p1[...] = jnp.zeros_like(p1)
    edge_u = r["edge_u"]
    edge_u[...] = jnp.zeros_like(edge_u)
    for copy in smalls:
        copy.wait()
    columns = []
    for layer in range(2):
        small[layer, 0:taps, 0 : 2 * STATE] = conv_weight[layer, :, inner : inner + 2 * STATE]
        small[layer, 4:5, 0 : 2 * STATE] = conv_bias[layer : layer + 1, inner : inner + 2 * STATE]
        small[layer, 5:6, 0:HEADS] = r["step_bias"][layer : layer + 1, :]
        small[layer, 6:7, 0:HEADS] = r["decay_log"][layer : layer + 1, :]
        small[layer, 7:8, 0:HEADS] = r["skip_gain"][layer : layer + 1, :]
        r["state_w"][layer] = r["state_weight"][:, layer, :]
        turned = jnp.transpose(small[layer])
        columns.append([turned[0:STATE, 5 + i : 6 + i] for i in range(3)])

    def project(layer, u):
        normed = rms(u.astype(F32), norm_gain[layer : layer + 1, :]).astype(BF16)
        x = dot(normed, in_w[layer, :, inner:]).astype(BF16).astype(F32)
        p = dot_nt(normed, r["state_w"][layer]).astype(BF16).astype(F32)
        return normed, x, p

    def gate(layer, normed):
        return silu(dot(normed, in_w[layer, :, :inner]).astype(BF16).astype(F32))

    xc_ref, y_ref = r["xc"], r["y"]

    def conv_parts(layer, start, size, window_x, window_p, raw):
        for i in range(inner // LANES):
            at = slice(i * LANES, (i + 1) * LANES)
            total = jnp.broadcast_to(conv_bias[layer : layer + 1, at], (size, LANES))
            for k in range(taps):
                total = total + conv_weight[layer, k : k + 1, at] * window_x(k, at)
            xc_ref[start : start + size, at] = silu(total).astype(BF16)
        total = jnp.broadcast_to(small[layer, 4:5, :], (size, LANES))
        for k in range(taps):
            total = total + small[layer, k : k + 1, :] * window_p(k)
        lane = iota((size, LANES), 1)
        bc = silu(total).astype(BF16).astype(F32)
        turned = jnp.transpose(jnp.where(lane < 2 * STATE, bc, raw))
        c_side = jnp.where((lane >= STATE) & (lane < 2 * STATE), bc, 0.0).astype(BF16)
        return turned, c_side

    def before(layer, backward, groups, size, loader, score_ref, sum_ref, sent):
        bias, decay_col, _ = columns[layer]
        rate_scale = -jnp.exp(decay_col) * LOG2E
        last_at = 0 if backward else size - 1
        sequence = list(range(groups))[:: -1 if backward else 1]
        carried, total_last, kept = None, None, {}
        for g in sequence:
            start = g * size
            window_x, window_p, raw = loader(g)
            turned, c_side = conv_parts(layer, start, size, window_x, window_p, raw)
            b_rows, c_rows = turned[0:STATE], turned[STATE : 2 * STATE]
            raw_rows = turned[2 * STATE : 3 * STATE] + bias
            step = jnp.maximum(raw_rows, 0.0) + jnp.log1p(jnp.exp(-jnp.abs(raw_rows)))
            rate = step * rate_scale
            high = rate.astype(BF16)
            low = (rate - high.astype(F32)).astype(BF16)
            both = dot(jnp.concatenate([high, low], axis=0), sum_ref[...])
            cum = both[0:STATE] + both[STATE : 2 * STATE]
            less = cum - jnp.log2(step)
            last = cum[:, last_at : last_at + 1]
            tail = jnp.exp2(last - less)
            weighted = jnp.concatenate(
                [b_rows * tail[h : h + 1, :] for h in range(HEADS)], axis=0
            ).astype(BF16)
            heads_per = 256 // HEADDIM
            parts = []
            for i in range(inner // 256):
                got = dot(
                    weighted[i * heads_per * STATE : (i + 1) * heads_per * STATE],
                    xc_ref[start : start + size, i * 256 : (i + 1) * 256],
                )
                lane = iota((STATE, 256), 1) // HEADDIM
                part = jnp.zeros((STATE, 256), F32)
                for h in range(heads_per):
                    part = jnp.where(lane == h, got[h * STATE : (h + 1) * STATE], part)
                parts.append(part)
            local = jnp.concatenate(parts, axis=1)
            grown_last = spread(jnp.exp2(last))
            r["local"][g] = local
            r["grown_last"][g : g + 1, :] = grown_last
            carried = local if carried is None else grown_last * carried + local
            total_last = last if total_last is None else total_last + last
            both_b = [b_rows, b_rows, jnp.zeros((LANES - 2 * STATE, size), F32)]
            score_ref[start : start + size, :] = dot(
                c_side, jnp.concatenate(both_b, axis=0).astype(BF16)
            )
            kept[g] = (c_rows, cum, less)
        decay = jnp.exp2(total_last)
        decay_high = decay.astype(BF16).astype(F32)
        lane = iota((STATE, LANES), 1)
        sent[:, 0:inner] = carried.astype(BF16)
        sent[:, inner : inner + LANES] = jnp.where(
            lane == 0, decay_high, jnp.where(lane == 1, decay - decay_high, 0.0)
        ).astype(BF16)
        return sequence, kept

    def state_copy(layer, source, j):
        return remote(
            r["sent"].at[layer],
            r["gathered"].at[layer, source],
            r["gs"].at[layer, j],
            r["gr"].at[layer, source],
            j,
        )

    def send_state(layer, backward):
        for j in list(range(n))[:: 1 if backward else -1]:

            @pl.when((me > j) if backward else (me < j))
            def _():
                state_copy(layer, me, j).start()

    def within(layer, sequence, kept, size, score_ref, neg_ref):
        skip = spread(columns[layer][2])
        even = iota((size, LANES), 1) < HEADDIM
        entering = {}
        for g in sequence:
            here = slice(g * size, (g + 1) * size)
            c_rows, cum, less = kept[g]
            grown = jnp.exp2(cum)
            stack = [c_rows * grown[h : h + 1, :] for h in range(HEADS)] + [cum]
            stack.append(jnp.zeros((-STATE * (HEADS + 1) % LANES, size), F32))
            turned = jnp.transpose(jnp.concatenate(stack, axis=0))
            entering[g] = turned[:, 0 : HEADS * STATE].astype(BF16)
            scores = score_ref[here, :]
            for pair in range(HEADS // 2):
                at = slice(pair * LANES, (pair + 1) * LANES)
                xp = xc_ref[here, at]
                weights = []
                for h in (2 * pair, 2 * pair + 1):
                    column = turned[:, HEADS * STATE + h : HEADS * STATE + h + 1]
                    diff = (column - less[h : h + 1, :]) + neg_ref[...]
                    weights.append((scores * jnp.exp2(diff)).astype(BF16))
                zero = jnp.zeros_like(xp)
                stacked = jnp.concatenate(
                    [jnp.where(even, xp, zero), jnp.where(even, zero, xp)], axis=0
                )
                y_ref[here, at] = skip[:, at] * xp.astype(F32) + dot(
                    jnp.concatenate(weights, axis=1), stacked
                )
        return entering

    def arrived(layer, backward):
        arrive = r["arrive"]
        arrive[...] = jnp.zeros_like(arrive)
        gathered = r["gathered"]
        for i in list(range(n))[:: -1 if backward else 1]:

            @pl.when((me < i) if backward else (me > i))
            def _():
                state_copy(layer, i, (i + 1) % n).wait_recv()
                factor = jnp.sum(
                    gathered[layer, i, :, inner : inner + LANES].astype(F32), axis=1, keepdims=True
                )
                arrive[...] = spread(factor) * arrive[...] + gathered[layer, i, :, 0:inner].astype(
                    F32
                )

        return arrive[...]

    def step_out(g, entering, state):
        low = state.astype(BF16)
        wide = jnp.concatenate([low] * HEADS, axis=0) * diag[...]
        inter = dot(entering[g], wide)
        return inter, r["grown_last"][g : g + 1, :] * state + r["local"][g]

    def finish(layer, y, sz, token):
        mixed = rms(y * sz, out_gain[layer : layer + 1, :]).astype(BF16)
        return (token.astype(F32) + dot(mixed, out_w[layer])).astype(BF16)

    x0, z0 = r["x0"], r["z0"]
    weights[0].wait()
    last_normed = None
    for k in range(chips):
        source = xor(chip, k, bits - 1)
        if k == 0:
            own.wait()
            first_copy(1).wait_recv()
        else:
            first_copy(2 * k).wait_recv()
            first_copy(2 * k + 1).wait_recv()
        at = pl.ds(source * 2 * rows, 2 * rows)
        normed, x, p = project(0, r1[at].reshape(2 * rows * block, width))
        x0[at] = x.reshape(2 * rows, block, inner)
        p0[at, :, 0:proj] = p.reshape(2 * rows, block, proj)
        if k < chips - 1:
            z0[at] = gate(0, normed).reshape(2 * rows, block, inner)
        else:
            last_normed, last_at = normed, at

    for source in range(sources):

        @pl.when((me != source) & (me < n - 1))
        def _():
            edge1_copy(source, 0 if source else 1).wait_recv()

    for i in range(taps - 1):
        line = edge1[i // rows].astype(F32)
        for q in range(pieces):
            j = (i % rows) * pieces + q
            edge_u[i : i + 1, q * LANES : (q + 1) * LANES] = line[j : j + 1, :]
    _, edge_x, edge_p = project(0, edge_u[...].astype(BF16))
    edge_p = jnp.concatenate([edge_p, jnp.zeros((EDGE, LANES - proj), F32)], axis=1)
    for i in range(taps - 1):
        for ref, line in ((x0, edge_x), (p0, edge_p)):
            wide = ref.shape[2]
            moved = pltpu.roll(ref[i], block - 1, 0)
            final = iota((block, wide), 0) == block - 1
            ref[full + i] = jnp.where(final, line[i : i + 1, :], moved)

    groups0 = block // SUB

    def loader0(g):
        at_g = slice(g * SUB, (g + 1) * SUB)

        def window_x(k, at):
            first = taps - 1 - k
            return x0[first : first + full, at_g, at].reshape(size0, LANES)

        def window_p(k):
            first = taps - 1 - k
            return p0[first : first + full, at_g, :].reshape(size0, LANES)

        return window_x, window_p, p0[0:full, at_g, :].reshape(size0, LANES)

    sequence, kept = before(
        0, True, groups0, size0, loader0, r["score0"], r["sum0"], r["sent"].at[0]
    )
    send_state(0, True)
    z0[last_at] = gate(0, last_normed).reshape(2 * rows, block, inner)
    entering = within(0, sequence, kept, size0, r["score0"], r["neg0"])
    state = arrived(0, True)
    weights[2].wait()

    def second_copy(chunk, mask):
        to = xor(me, mask, bits)
        return remote(
            o1.at[at_rows(to), chunk * ocols : (chunk + 1) * ocols, :],
            r2.at[:, pl.ds(pl.multiple_of(me * block + chunk * ocols, ocols), ocols), :],
            r["s2"].at[chunk, mask],
            r["v2"].at[chunk, mask],
            to,
        )

    def own2_copy(chunk):
        return pltpu.make_async_copy(
            o1.at[at_rows(me), chunk * ocols : (chunk + 1) * ocols, :],
            r2.at[:, pl.ds(pl.multiple_of(me * block + chunk * ocols, ocols), ocols), :],
            r["l_sem"].at[1 + chunk],
        )

    def edge2_copy(j):
        return remote(
            o1.at[rows * j - 1, pl.ds(block - edge, edge), :],
            edge2,
            r["e2s"].at[j],
            r["e2r"],
            j,
        )

    edge2_own = pltpu.make_async_copy(
        o1.at[rows * (n - 1) - 1, pl.ds(block - edge, edge), :], edge2, r["l_sem"].at[1 + chunks]
    )

    for chunk in reversed(range(chunks)):
        ys = []
        for g in reversed(range(chunk * ocols // SUB, (chunk + 1) * ocols // SUB)):
            inter, state = step_out(g, entering, state)
            y = y_ref[g * size0 : (g + 1) * size0, :] + inter
            ys.insert(0, y.reshape(full, SUB, inner))
        at = slice(chunk * ocols, (chunk + 1) * ocols)
        flat = full * ocols
        y = jnp.concatenate(ys, axis=1).reshape(flat, inner)
        after = finish(0, y, z0[:, at, :].reshape(flat, inner), r1[:, at, :].reshape(flat, width))
        o1[:, at, :] = after.reshape(full, ocols, width)
        for mask in range(n - 1, 0, -1):
            second_copy(chunk, mask).start()
        own2_copy(chunk).start()
        if chunk == chunks - 1:

            @pl.when(me == n - 1)
            def _():
                for j in range(1, n - 1):
                    edge2_copy(j).start()
                edge2_own.start()

    x1, z1 = r["x1"], r["z1"]
    weights[1].wait()
    pair = 2 * block
    for k in range(chips):
        source = xor(chip, k, bits - 1)
        for chunk in reversed(range(chunks)):
            if k == 0:
                own2_copy(chunk).wait()
                second_copy(chunk, 1).wait_recv()
            else:
                second_copy(chunk, 2 * k).wait_recv()
                second_copy(chunk, 2 * k + 1).wait_recv()
        at = pl.ds(pl.multiple_of(source * pair, pair), pair)
        normed, x, p = project(1, r2[:, at, :].reshape(rows * pair, width))
        for i in range(rows):
            from_row = slice(i * pair, (i + 1) * pair)
            to_row = pl.ds(pl.multiple_of(EDGE + i * cols + source * pair, SUB), pair)
            x1[to_row, :] = x[from_row]
            p1[to_row, 0:proj] = p[from_row]
        if k < chips - 1:
            sz = gate(1, normed)
            for i in range(rows):
                to_row = pl.ds(pl.multiple_of(i * cols + source * pair, SUB), pair)
                z1[to_row, :] = sz[i * pair : (i + 1) * pair]
        else:
            last_normed = normed

    @pl.when((me > 0) & (me < n - 1))
    def _():
        edge2_copy(1).wait_recv()

    @pl.when(me == n - 1)
    def _():
        edge2_own.wait()

    edge_in = edge2[...]
    if edge < EDGE:
        edge_in = jnp.concatenate([jnp.zeros((EDGE - edge, width), BF16), edge_in], axis=0)
    _, edge_x, edge_p = project(1, edge_in)
    x1[0:EDGE, :] = edge_x
    p1[0:EDGE, 0:proj] = edge_p

    groups1 = tokens // size1

    def loader1(g):
        first = EDGE - (taps - 1) + g * size1

        def window_x(k, at):
            return x1[first + k : first + k + size1, at]

        def window_p(k):
            return p1[first + k : first + k + size1, :]

        return window_x, window_p, p1[EDGE + g * size1 : EDGE + (g + 1) * size1, :]

    sequence, kept = before(
        1, False, groups1, size1, loader1, r["score1"], r["sum1"], r["sent"].at[1]
    )
    send_state(1, False)
    sz = gate(1, last_normed)
    source = xor(chip, chips - 1, bits - 1)
    for i in range(rows):
        to_row = pl.ds(pl.multiple_of(i * cols + source * pair, SUB), pair)
        z1[to_row, :] = sz[i * pair : (i + 1) * pair]
    entering = within(1, sequence, kept, size1, r["score1"], r["neg1"])
    state = arrived(1, False)
    per_row = groups1 // rows
    for i in range(rows):
        ys = []
        for g in range(i * per_row, (i + 1) * per_row):
            inter, state = step_out(g, entering, state)
            ys.append(y_ref[g * size1 : (g + 1) * size1, :] + inter)
        y = jnp.concatenate(ys, axis=0)
        out[i] = finish(1, y, z1[i * cols : (i + 1) * cols, :], r2[i])

    for mask in range(1, n):
        first_copy(mask).wait_send()
        for chunk in range(chunks):
            second_copy(chunk, mask).wait_send()
    for layer in range(2):
        for j in range(n):

            @pl.when((me > j) if layer == 0 else (me < j))
            def _():
                state_copy(layer, me, j).wait_send()

    for source in range(sources):

        @pl.when(me == source)
        def _():
            for j in range(n - 1):
                if j != source:
                    edge1_copy(source, j).wait_send()

    @pl.when(me == n - 1)
    def _():
        for j in range(1, n - 1):
            edge2_copy(j).wait_send()


def on_device(n, *arrays):
    slide, in_weight, out_weight = arrays[0], arrays[2], arrays[10]
    rows, cols, width = slide.shape
    full, block, tokens = rows * n, cols // n, rows * cols
    inner = in_weight.shape[2] // 2
    edge = min(EDGE, block)
    taps = arrays[4].shape[1]
    sources = -(-(taps - 1) // rows)
    chunks = block // min(16, block)
    size0, size1 = full * SUB, min(LANES, cols)
    groups = max(tokens // size0, tokens // size1)
    state_weight = jnp.transpose(arrays[3], (2, 0, 1))
    operands = dict(
        slide=slide,
        norm_gain_hbm=arrays[1],
        in_hbm=in_weight,
        state_weight_hbm=state_weight,
        conv_weight_hbm=arrays[4],
        conv_bias_hbm=arrays[5],
        step_bias_hbm=arrays[6],
        decay_log_hbm=arrays[7],
        skip_gain_hbm=arrays[8],
        out_gain_hbm=arrays[9],
        out_hbm=out_weight,
    )
    dma = pltpu.SemaphoreType.DMA
    vmem = pltpu.VMEM
    scratch = dict(
        slide_v=vmem(slide.shape, BF16),
        in_w=vmem(in_weight.shape, BF16),
        out_w=vmem(out_weight.shape, BF16),
        norm_gain=vmem(arrays[1].shape, F32),
        state_weight=vmem(state_weight.shape, BF16),
        conv_weight=vmem(arrays[4].shape, F32),
        conv_bias=vmem(arrays[5].shape, F32),
        step_bias=vmem(arrays[6].shape, F32),
        decay_log=vmem(arrays[7].shape, F32),
        skip_gain=vmem(arrays[8].shape, F32),
        out_gain=vmem(arrays[9].shape, F32),
        state_w=vmem((2, state_weight.shape[0], width), BF16),
        small=vmem((2, 8, LANES), F32),
        packf=vmem((n, EDGE, LANES), F32),
        pack=vmem((n, EDGE, LANES), BF16),
        edge1=vmem((sources, EDGE, LANES), BF16),
        edge2=vmem((edge, width), BF16),
        edge_u=vmem((EDGE, width), F32),
        r1=vmem((full, block, width), BF16),
        o1=vmem((full, block, width), BF16),
        r2=vmem((rows, cols, width), BF16),
        x0=vmem((full + taps - 1, block, inner), F32),
        p0=vmem((full + taps - 1, block, LANES), F32),
        z0=vmem((full, block, inner), F32),
        x1=vmem((tokens + EDGE, inner), F32),
        p1=vmem((tokens + EDGE, LANES), F32),
        z1=vmem((tokens, inner), F32),
        xc=vmem((tokens, inner), BF16),
        y=vmem((tokens, inner), F32),
        score0=vmem((tokens, size0), F32),
        score1=vmem((tokens, size1), F32),
        neg0=vmem((size0, size0), F32),
        neg1=vmem((size1, size1), F32),
        sum0=vmem((size0, size0), BF16),
        sum1=vmem((size1, size1), BF16),
        diag=vmem((HEADS * STATE, inner), BF16),
        local=vmem((groups, STATE, inner), F32),
        grown_last=vmem((SUB, inner), F32),
        sent=vmem((2, STATE, inner + LANES), BF16),
        gathered=vmem((2, n, STATE, inner + LANES), BF16),
        arrive=vmem((STATE, inner), F32),
        w_sem=dma((12,)),
        l_sem=dma((2 + chunks,)),
        s1=dma((n,)),
        v1=dma((n,)),
        e1s=dma((n,)),
        e1r=dma((sources,)),
        s2=dma((chunks, n)),
        v2=dma((chunks, n)),
        e2s=dma((n,)),
        e2r=dma,
        gs=dma((2, n)),
        gr=dma((2, n)),
    )
    names = list(operands) + ["out"] + list(scratch)
    return pl.pallas_call(
        functools.partial(kernel, n, names),
        out_shape=vmem((rows, cols, width), BF16),
        in_specs=[pl.BlockSpec(memory_space=pl.ANY)] * len(operands),
        out_specs=pl.BlockSpec(memory_space=vmem),
        scratch_shapes=list(scratch.values()),
        compiler_params=pltpu.CompilerParams(
            collective_id=0, has_side_effects=True, vmem_limit_bytes=56 * 1024 * 1024
        ),
    )(*operands.values())


def solution(mesh):
    placed = (P(("dp", "seq"), None, None),) + (P(),) * 10
    return jax.shard_map(
        functools.partial(on_device, mesh.shape["seq"]),
        mesh=mesh,
        in_specs=placed,
        out_specs=P(("dp", "seq"), None, None),
        check_vma=False,
    )
```

```python
import functools
import math

import jax
import jax.numpy as jnp
from jax import lax
from jax.experimental import pallas as pl
from jax.experimental.pallas import tpu as pltpu
from jax.sharding import PartitionSpec as P

HEADS = 12
HEADDIM = 64
STATE = 16
LANES = 128
SUB = 8
EDGE = 16
EPS = 1e-05
LOG2E = math.log2(math.e)
MESH = pl.DeviceIdType.MESH
F32 = jnp.float32
BF16 = jnp.bfloat16


def silu(v):
    half = 0.5 * v
    return half + half * jnp.tanh(half)


def rms(v, gain):
    return v * lax.rsqrt(jnp.mean(v * v, axis=-1, keepdims=True) + EPS) * gain


def iota(shape, dim):
    return lax.broadcasted_iota(jnp.int32, shape, dim)


def dot(a, b):
    return jnp.dot(a, b, preferred_element_type=F32)


def dot_nt(a, b):
    return lax.dot_general(a, b, (((1,), (1,)), ((), ())), preferred_element_type=F32)


def xor(a, b, bits):
    total = 0
    for i in range(bits):
        total = total + lax.rem(a // 2**i + b // 2**i, 2) * 2**i
    return total


def kernel(n, names, *all_refs):
    r = dict(zip(names, all_refs))
    out = r["out"]
    slide, in_hbm, out_hbm = r["slide"], r["in_hbm"], r["out_hbm"]
    me = lax.axis_index("seq")
    rows, cols, width = slide.shape
    full = rows * n
    block = cols // n
    tokens = rows * cols
    inner = in_hbm.shape[2] // 2
    taps = r["conv_weight_hbm"].shape[1]
    proj = r["state_weight_hbm"].shape[0]
    bits = n.bit_length() - 1
    chips = n // 2
    chip = me // 2
    sources = -(-(taps - 1) // rows)
    pieces = width // LANES
    edge = min(EDGE, block)
    ocols = min(16, block)
    chunks = block // ocols
    size0 = full * SUB
    size1 = min(LANES, cols)
    lines1 = size1 // SUB
    part = 256
    parts = inner // part

    def remote(src, dst, send_sem, recv_sem, to):
        return pltpu.make_async_remote_copy(
            src_ref=src,
            dst_ref=dst,
            send_sem=send_sem,
            recv_sem=recv_sem,
            device_id={"seq": to},
            device_id_type=MESH,
        )

    barrier = pltpu.get_barrier_semaphore()
    for k in range(1, n):
        pl.semaphore_signal(
            barrier, inc=1, device_id={"seq": lax.rem(me + k, n)}, device_id_type=MESH
        )

    w_sem = r["w_sem"]
    local_in = [pltpu.make_async_copy(slide, r["slide_v"], w_sem.at[0])]
    small_names = [name[:-4] for name in names if name.endswith("_hbm") and name[:-4] in names]
    small_names = [name for name in small_names if name not in ("in", "out")]
    smalls = [
        pltpu.make_async_copy(r[name + "_hbm"], r[name], w_sem.at[1 + i])
        for i, name in enumerate(small_names)
    ]
    base = 1 + len(small_names)
    weights = [
        pltpu.make_async_copy(in_hbm.at[0], r["in_w"].at[0], w_sem.at[base]),
        pltpu.make_async_copy(in_hbm.at[1], r["in_w"].at[1], w_sem.at[base + 1]),
        pltpu.make_async_copy(out_hbm, r["out_w"], w_sem.at[base + 2]),
    ]
    local_in[0].start()
    for copy in smalls:
        copy.start()
    weights[0].start()
    weights[2].start()
    weights[1].start()

    norm_gain, conv_weight, conv_bias = r["norm_gain"], r["conv_weight"], r["conv_bias"]
    in_w, out_w, out_gain = r["in_w"], r["out_w"], r["out_gain"]
    slide_v, r1, r2, o1 = r["slide_v"], r["r1"], r["r2"], r["o1"]
    edge1, edge2, pack = r["edge1"], r["edge2"], r["pack"]

    def at_cols(j):
        return pl.ds(pl.multiple_of(j * block, block), block)

    def at_rows(j):
        return pl.ds(j * rows, rows)

    local_in[0].wait()
    packf = r["packf"]
    packf[...] = jnp.zeros_like(packf)
    for j in range(n - 1):
        for i in range(rows):
            at = (j + 1) * block
            line = slide_v[i, at : at + SUB, :].astype(F32)
            for q in range(pieces):
                packf[j, i * pieces + q : i * pieces + q + 1, :] = line[
                    0:1, q * LANES : (q + 1) * LANES
                ]
    pack[...] = packf[...].astype(BF16)

    r["gathered"][...] = jnp.zeros_like(r["gathered"])
    pl.semaphore_wait(barrier, n - 1)

    def first_copy(mask):
        to = xor(me, mask, bits)
        return remote(
            slide_v.at[:, at_cols(to), :],
            r1.at[at_rows(me)],
            r["s1"].at[mask],
            r["v1"].at[mask],
            to,
        )

    for mask in range(1, n):
        first_copy(mask).start()

    def edge1_copy(source, j):
        return remote(
            pack.at[j],
            edge1.at[source],
            r["e1s"].at[j],
            r["e1r"].at[source],
            j,
        )

    for source in range(sources):

        @pl.when(me == source)
        def _():
            for j in range(n - 1):
                if j != source:
                    edge1_copy(source, j).start()
            edge1[source] = pack[source]

    own = pltpu.make_async_copy(slide_v.at[:, at_cols(me), :], r1.at[at_rows(me)], r["l_sem"].at[0])
    own.start()

    @pl.when(me == n - 1)
    def _():
        edge1[...] = jnp.zeros_like(edge1)

    @pl.when(me == 0)
    def _():
        edge2[...] = jnp.zeros_like(edge2)

    head_mask = iota((STATE, inner), 0) == iota((STATE, inner), 1) // HEADDIM

    def spread(column):
        return jnp.sum(jnp.where(head_mask, column, 0.0), axis=0, keepdims=True)

    diag = r["diag"]
    diag[...] = jnp.where(
        iota((HEADS * STATE, inner), 0) // STATE == iota((HEADS * STATE, inner), 1) // HEADDIM,
        1.0,
        0.0,
    ).astype(BF16)

    def key(v, lines):
        return lax.rem(v, SUB) * lines + v // SUB

    order0 = [key(iota((size0, size0), i), full) for i in range(2)]
    order1 = [key(iota((size1, size1), i), lines1) for i in range(2)]
    r["neg0"][...] = jnp.where(order0[1] >= order0[0], 0.0, -jnp.inf)
    r["sum0"][...] = jnp.where(order0[0] >= order0[1], 1.0, 0.0).astype(BF16)
    r["neg1"][...] = jnp.where(order1[1] <= order1[0], 0.0, -jnp.inf)
    r["sum1"][...] = jnp.where(order1[0] <= order1[1], 1.0, 0.0).astype(BF16)

    small = r["small"]
    small[...] = jnp.zeros_like(small)
    p0, p1 = r["p0"], r["p1"]
    p0[...] = jnp.zeros_like(p0)
    p1[...] = jnp.zeros_like(p1)
    edge_u = r["edge_u"]
    edge_u[...] = jnp.zeros_like(edge_u)
    for copy in smalls:
        copy.wait()
    columns = []
    for layer in range(2):
        small[layer, 0:taps, 0 : 2 * STATE] = conv_weight[layer, :, inner : inner + 2 * STATE]
        small[layer, 4:5, 0 : 2 * STATE] = conv_bias[layer : layer + 1, inner : inner + 2 * STATE]
        small[layer, 5:6, 0:HEADS] = r["step_bias"][layer : layer + 1, :]
        small[layer, 6:7, 0:HEADS] = r["decay_log"][layer : layer + 1, :]
        small[layer, 7:8, 0:HEADS] = r["skip_gain"][layer : layer + 1, :]
        r["state_w"][layer] = r["state_weight"][:, layer, :]
        turned = jnp.transpose(small[layer])
        columns.append([turned[0:STATE, 5 + i : 6 + i] for i in range(3)])

    def project(layer, u):
        normed = rms(u.astype(F32), norm_gain[layer : layer + 1, :]).astype(BF16)
        x = dot(normed, in_w[layer, :, inner:]).astype(BF16).astype(F32)
        p = dot_nt(normed, r["state_w"][layer]).astype(BF16).astype(F32)
        return normed, x, p

    def gate(layer, normed):
        return silu(dot(normed, in_w[layer, :, :inner]).astype(BF16).astype(F32))

    xc_ref, y0, y1, ent1 = r["xc"], r["y0"], r["y1"], r["ent1"]

    def state_copy(layer, i, source, to):
        wide = part + LANES if i == 0 else part
        return remote(
            r["sent"].at[layer, i, :, 0:wide],
            r["gathered"].at[layer, source, i, :, 0:wide],
            r["gs"].at[layer, i, to],
            r["gr"].at[layer, i, source],
            to,
        )

    def later(i, j, backward):
        return (i > j) if backward else (i < j)

    def before(layer, backward, groups, size, load_p, load_x, sum_ref):
        bias, decay_col, _ = columns[layer]
        rate_scale = -jnp.exp(decay_col) * LOG2E
        last_at = 0 if backward else size - 1
        sequence = list(range(groups))[:: -1 if backward else 1]
        turned, c_side = {}, {}
        lane = iota((size, LANES), 1)
        for g in sequence:
            windows = load_p(g)
            total = small[layer, 4:5, :] + small[layer, 0:1, :] * windows[0]
            for k in range(1, taps):
                total = total + small[layer, k : k + 1, :] * windows[k]
            bc = silu(total).astype(BF16).astype(F32)
            turned[g] = jnp.transpose(jnp.where(lane < 2 * STATE, bc, windows[-1]))
            c_side[g] = jnp.where((lane >= STATE) & (lane < 2 * STATE), bc, 0.0).astype(BF16)
        raw = bias + jnp.concatenate(
            [turned[g][2 * STATE : 3 * STATE] for g in sequence], axis=1
        )
        step = jnp.maximum(raw, 0.0) + jnp.log1p(jnp.exp(-jnp.abs(raw)))
        rate = step * rate_scale
        high = rate.astype(BF16)
        low = (rate - high.astype(F32)).astype(BF16)
        split = jnp.concatenate([high, low], axis=0)
        log_step = jnp.log2(step)
        total_last, kept, weighted, grown_last = None, {}, {}, {}
        for i, g in enumerate(sequence):
            at = slice(i * size, (i + 1) * size)
            both = dot(split[:, at], sum_ref[...])
            cum = both[0:STATE] + both[STATE : 2 * STATE]
            less = cum - log_step[:, at]
            last = cum[:, last_at : last_at + 1]
            tail = jnp.exp2(last - less)
            b_rows = turned[g][0:STATE]
            weighted[g] = jnp.concatenate(
                [b_rows * tail[h : h + 1, :] for h in range(HEADS)], axis=0
            ).astype(BF16)
            grown_last[g] = spread(jnp.exp2(last))
            r["grown_last"][g : g + 1, :] = grown_last[g]
            total_last = last if total_last is None else total_last + last
            kept[g] = (turned[g], c_side[g], cum, less)
        decay = jnp.exp2(total_last)
        decay_high = decay.astype(BF16).astype(F32)
        lane = iota((STATE, LANES), 1)
        sent = r["sent"]
        sent[layer, 0, :, part : part + LANES] = jnp.where(
            lane == 0, decay_high, jnp.where(lane == 1, decay - decay_high, 0.0)
        ).astype(BF16)
        heads_per = part // HEADDIM
        lane = iota((STATE, part), 1) // HEADDIM
        for i in range(parts):
            whole = slice(i * part, (i + 1) * part)
            carried = None
            for g in sequence:
                here = slice(g * size, (g + 1) * size)
                for q in range(i * part // LANES, (i + 1) * part // LANES):
                    at = slice(q * LANES, (q + 1) * LANES)
                    windows = load_x(g, q)
                    total = conv_bias[layer : layer + 1, at] + (
                        conv_weight[layer, 0:1, at] * windows[0]
                    )
                    for k in range(1, taps):
                        total = total + conv_weight[layer, k : k + 1, at] * windows[k]
                    xc_ref[here, at] = silu(total).astype(BF16)
                got = dot(
                    weighted[g][i * heads_per * STATE : (i + 1) * heads_per * STATE],
                    xc_ref[here, whole],
                )
                local = got[0:STATE]
                for h in range(1, heads_per):
                    local = jnp.where(lane == h, got[h * STATE : (h + 1) * STATE], local)
                r["local"][g, :, whole] = local
                carried = local if carried is None else grown_last[g][:, whole] * carried + local
            sent[layer, i, :, 0:part] = carried.astype(BF16)
            for to in list(range(n))[:: 1 if backward else -1]:

                @pl.when(later(me, to, backward))
                def _():
                    state_copy(layer, i, me, to).start()

        return sequence, kept

    def within(layer, sequence, kept, size, neg_ref):
        skip = spread(columns[layer][2])
        even = iota((size, LANES), 1) < HEADDIM
        entering = {}
        for g in sequence:
            here = slice(g * size, (g + 1) * size)
            turned, c_side, cum, less = kept[g]
            b_rows, c_rows = turned[0:STATE], turned[STATE : 2 * STATE]
            both_b = [b_rows, b_rows, jnp.zeros((LANES - 2 * STATE, size), F32)]
            scores = dot(c_side, jnp.concatenate(both_b, axis=0).astype(BF16))
            grown = jnp.exp2(cum)
            stack = [c_rows * grown[h : h + 1, :] for h in range(HEADS)] + [cum]
            stack.append(jnp.zeros((-STATE * (HEADS + 1) % LANES, size), F32))
            across = jnp.transpose(jnp.concatenate(stack, axis=0))
            if layer == 0:
                entering[g] = across[:, 0 : HEADS * STATE].astype(BF16)
            else:
                for q in range(2):
                    for i in range(lines1):
                        ent1[q, pl.ds(g * size + i, SUB, stride=lines1), :] = across[
                            i * SUB : (i + 1) * SUB, q * LANES : (q + 1) * LANES
                        ]
            for pair in range(HEADS // 2):
                at = slice(pair * LANES, (pair + 1) * LANES)
                xp = xc_ref[here, at]
                weights = []
                for h in (2 * pair, 2 * pair + 1):
                    column = across[:, HEADS * STATE + h : HEADS * STATE + h + 1]
                    diff = (column - less[h : h + 1, :]) + neg_ref[...]
                    weights.append((scores * jnp.exp2(diff)).astype(BF16))
                zero = jnp.zeros_like(xp)
                stacked = jnp.concatenate(
                    [jnp.where(even, xp, zero), jnp.where(even, zero, xp)], axis=0
                )
                y = skip[:, at] * xp.astype(F32) + dot(jnp.concatenate(weights, axis=1), stacked)
                if layer == 0:
                    y0[here, at] = y
                else:
                    for i in range(lines1):
                        y1[pair, pl.ds(g * size + i, SUB, stride=lines1), :] = y[
                            i * SUB : (i + 1) * SUB
                        ]
        if layer == 1:
            for g in sequence:
                here = slice(g * size, (g + 1) * size)
                entering[g] = jnp.concatenate(
                    [ent1[0, here, :], ent1[1, here, 0 : HEADS * STATE - LANES]], axis=1
                ).astype(BF16)
        return entering

    def arrived(layer, backward):
        gathered = r["gathered"]
        factors, state = {}, []
        order = list(range(n))[:: -1 if backward else 1]
        for i in range(parts):
            whole = slice(i * part, (i + 1) * part)
            for source in order:

                @pl.when(later(source, me, backward))
                def _():
                    state_copy(layer, i, source, (source + 1) % n).wait_recv()

            total = jnp.zeros((STATE, part), F32)
            for source in order:
                valid = later(source, me, backward)
                if i == 0:
                    packed = gathered[layer, source, 0, :, part : part + LANES].astype(F32)
                    factor = spread(jnp.sum(packed, axis=1, keepdims=True))
                    factors[source] = jnp.where(valid, factor, 1.0)
                came = gathered[layer, source, i, :, 0:part].astype(F32)
                total = factors[source][:, whole] * total + jnp.where(valid, came, 0.0)
            state.append(total)
        return jnp.concatenate(state, axis=1)

    def step_out(g, entering, state):
        low = state.astype(BF16)
        wide = jnp.concatenate([low] * HEADS, axis=0) * diag[...]
        inter = dot(entering[g], wide)
        return inter, r["grown_last"][g : g + 1, :] * state + r["local"][g]

    def finish(layer, y, sz, token):
        gated = y * sz
        scale = lax.rsqrt(jnp.mean(gated * gated, axis=-1, keepdims=True) + EPS)
        mixed = (gated * out_gain[layer : layer + 1, :]).astype(BF16)
        return (token.astype(F32) + scale * dot(mixed, out_w[layer])).astype(BF16)

    x0, z0 = r["x0"], r["z0"]
    weights[0].wait()
    last_normed = None
    for k in range(chips):
        source = xor(chip, k, bits - 1)
        if k == 0:
            own.wait()
            first_copy(1).wait_recv()
        else:
            first_copy(2 * k).wait_recv()
            first_copy(2 * k + 1).wait_recv()
        if k == chips - 1:
            for i in range(sources):

                @pl.when((me != i) & (me < n - 1))
                def _():
                    edge1_copy(i, 0 if i else 1).wait_recv()

            for i in range(taps - 1):
                line = edge1[i // rows].astype(F32)
                for q in range(pieces):
                    j = (i % rows) * pieces + q
                    edge_u[i : i + 1, q * LANES : (q + 1) * LANES] = line[j : j + 1, :]
        at = pl.ds(source * 2 * rows, 2 * rows)
        count = 2 * rows * block
        u = r1[at].reshape(count, width)
        if k == chips - 1:
            u = jnp.concatenate([u, edge_u[...].astype(BF16)], axis=0)
        normed, x, p = project(0, u)
        x0[at] = x[0:count].reshape(2 * rows, block, inner)
        p0[at, :, 0:proj] = p[0:count].reshape(2 * rows, block, proj)
        if k < chips - 1:
            z0[at] = gate(0, normed).reshape(2 * rows, block, inner)
        else:
            last_normed, last_at = normed[0:count], at
            edge_x = x[count:]
            edge_p = jnp.concatenate(
                [p[count:], jnp.zeros((EDGE, LANES - proj), F32)], axis=1
            )
    for i in range(taps - 1):
        for ref, line in ((p0, edge_p), (x0, edge_x)):
            wide = ref.shape[2]
            moved = pltpu.roll(ref[i], block - 1, 0)
            final = iota((block, wide), 0) == block - 1
            ref[full + i] = jnp.where(final, line[i : i + 1, :], moved)

    groups0 = block // SUB

    def windows0(ref, g, at):
        first = [taps - 1 - k for k in range(taps)]
        at_g = slice(g * SUB, (g + 1) * SUB)
        return [ref[i : i + full, at_g, at].reshape(size0, LANES) for i in first]

    sequence, kept = before(
        0,
        True,
        groups0,
        size0,
        lambda g: windows0(p0, g, slice(0, LANES)),
        lambda g, q: windows0(x0, g, slice(q * LANES, (q + 1) * LANES)),
        r["sum0"],
    )
    z0[last_at] = gate(0, last_normed).reshape(2 * rows, block, inner)
    entering = within(0, sequence, kept, size0, r["neg0"])
    state = arrived(0, True)
    weights[2].wait()

    def second_copy(chunk, mask):
        to = xor(me, mask, bits)
        return remote(
            o1.at[at_rows(to), chunk * ocols : (chunk + 1) * ocols, :],
            r2.at[:, pl.ds(pl.multiple_of(me * block + chunk * ocols, ocols), ocols), :],
            r["s2"].at[chunk, mask],
            r["v2"].at[chunk, mask],
            to,
        )

    def own2_copy(chunk):
        return pltpu.make_async_copy(
            o1.at[at_rows(me), chunk * ocols : (chunk + 1) * ocols, :],
            r2.at[:, pl.ds(pl.multiple_of(me * block + chunk * ocols, ocols), ocols), :],
            r["l_sem"].at[1 + chunk],
        )

    def edge2_copy(j):
        return remote(
            o1.at[rows * j - 1, pl.ds(block - edge, edge), :],
            edge2,
            r["e2s"].at[j],
            r["e2r"],
            j,
        )

    edge2_own = pltpu.make_async_copy(
        o1.at[rows * (n - 1) - 1, pl.ds(block - edge, edge), :], edge2, r["l_sem"].at[1 + chunks]
    )

    for chunk in reversed(range(chunks)):
        ys = []
        for g in reversed(range(chunk * ocols // SUB, (chunk + 1) * ocols // SUB)):
            inter, state = step_out(g, entering, state)
            y = y0[g * size0 : (g + 1) * size0, :] + inter
            ys.insert(0, y.reshape(full, SUB, inner))
        at = slice(chunk * ocols, (chunk + 1) * ocols)
        flat = full * ocols
        y = jnp.concatenate(ys, axis=1).reshape(flat, inner)
        after = finish(0, y, z0[:, at, :].reshape(flat, inner), r1[:, at, :].reshape(flat, width))
        o1[:, at, :] = after.reshape(full, ocols, width)
        for mask in range(1, n):
            second_copy(chunk, mask).start()
        own2_copy(chunk).start()
        if chunk == chunks - 1:

            @pl.when(me == n - 1)
            def _():
                for j in range(1, n - 1):
                    edge2_copy(j).start()
                edge2_own.start()

    x1, z1 = r["x1"], r["z1"]
    weights[1].wait()
    pair = 2 * block
    for k in range(chips):
        source = xor(chip, k, bits - 1)
        for chunk in reversed(range(chunks)):
            if k == 0:
                own2_copy(chunk).wait()
                second_copy(chunk, 1).wait_recv()
            else:
                second_copy(chunk, 2 * k).wait_recv()
                second_copy(chunk, 2 * k + 1).wait_recv()
        at = pl.ds(pl.multiple_of(source * pair, pair), pair)
        count = rows * pair
        u = r2[:, at, :].reshape(count, width)
        if k == chips - 1:

            @pl.when((me > 0) & (me < n - 1))
            def _():
                edge2_copy(1).wait_recv()

            @pl.when(me == n - 1)
            def _():
                edge2_own.wait()

            edge_in = edge2[...]
            if edge < EDGE:
                edge_in = jnp.concatenate([jnp.zeros((EDGE - edge, width), BF16), edge_in], axis=0)
            u = jnp.concatenate([u, edge_in], axis=0)
        normed, x, p = project(1, u)

        def put(to_row, from_row):
            p1[to_row, 0:proj] = p[from_row]
            for q in range(inner // LANES):
                x1[q, to_row, :] = x[from_row, q * LANES : (q + 1) * LANES]

        for i in range(rows):
            to_row = pl.ds(pl.multiple_of(EDGE + i * cols + source * pair, SUB), pair)
            put(to_row, slice(i * pair, (i + 1) * pair))
        if k < chips - 1:
            sz = gate(1, normed)
            for i in range(rows):
                to_row = pl.ds(pl.multiple_of(i * cols + source * pair, SUB), pair)
                z1[to_row, :] = sz[i * pair : (i + 1) * pair]
        else:
            last_normed = normed[0:count]
            put(slice(0, EDGE), slice(count, count + EDGE))

    groups1 = tokens // size1

    def windows1(ref, g, lead):
        first = EDGE - (taps - 1) + g * size1
        lines = [
            ref[lead + (pl.ds(first + i, SUB, stride=lines1), slice(None))]
            for i in range(lines1 + taps - 1)
        ]
        return [jnp.concatenate(lines[k : k + lines1], axis=0) for k in range(taps)]

    sequence, kept = before(
        1,
        False,
        groups1,
        size1,
        lambda g: windows1(p1, g, ()),
        lambda g, q: windows1(x1, g, (q,)),
        r["sum1"],
    )
    sz = gate(1, last_normed)
    source = xor(chip, chips - 1, bits - 1)
    for i in range(rows):
        to_row = pl.ds(pl.multiple_of(i * cols + source * pair, SUB), pair)
        z1[to_row, :] = sz[i * pair : (i + 1) * pair]
    entering = within(1, sequence, kept, size1, r["neg1"])
    state = arrived(1, False)
    per_row = groups1 // rows
    for i in range(rows):
        ys = []
        for g in range(i * per_row, (i + 1) * per_row):
            inter, state = step_out(g, entering, state)
            here = slice(g * size1, (g + 1) * size1)
            y = jnp.concatenate([y1[q, here, :] for q in range(inner // LANES)], axis=1)
            ys.append(y + inter)
        y = jnp.concatenate(ys, axis=0)
        out[i] = finish(1, y, z1[i * cols : (i + 1) * cols, :], r2[i])

    for mask in range(1, n):
        first_copy(mask).wait_send()
        for chunk in range(chunks):
            second_copy(chunk, mask).wait_send()
    for layer in range(2):
        for i in range(parts):
            for to in range(n):

                @pl.when(later(me, to, layer == 0))
                def _():
                    state_copy(layer, i, me, to).wait_send()


    for source in range(sources):

        @pl.when(me == source)
        def _():
            for j in range(n - 1):
                if j != source:
                    edge1_copy(source, j).wait_send()

    @pl.when(me == n - 1)
    def _():
        for j in range(1, n - 1):
            edge2_copy(j).wait_send()


def on_device(n, *arrays):
    slide, in_weight, out_weight = arrays[0], arrays[2], arrays[10]
    rows, cols, width = slide.shape
    full, block, tokens = rows * n, cols // n, rows * cols
    inner = in_weight.shape[2] // 2
    edge = min(EDGE, block)
    taps = arrays[4].shape[1]
    sources = -(-(taps - 1) // rows)
    chunks = block // min(16, block)
    size0, size1 = full * SUB, min(LANES, cols)
    groups = max(tokens // size0, tokens // size1)
    parts = inner // 256
    state_weight = jnp.transpose(arrays[3], (2, 0, 1))
    operands = dict(
        slide=slide,
        norm_gain_hbm=arrays[1],
        in_hbm=in_weight,
        state_weight_hbm=state_weight,
        conv_weight_hbm=arrays[4],
        conv_bias_hbm=arrays[5],
        step_bias_hbm=arrays[6],
        decay_log_hbm=arrays[7],
        skip_gain_hbm=arrays[8],
        out_gain_hbm=arrays[9],
        out_hbm=out_weight,
    )
    dma = pltpu.SemaphoreType.DMA
    vmem = pltpu.VMEM
    scratch = dict(
        slide_v=vmem(slide.shape, BF16),
        in_w=vmem(in_weight.shape, BF16),
        out_w=vmem(out_weight.shape, BF16),
        norm_gain=vmem(arrays[1].shape, F32),
        state_weight=vmem(state_weight.shape, BF16),
        conv_weight=vmem(arrays[4].shape, F32),
        conv_bias=vmem(arrays[5].shape, F32),
        step_bias=vmem(arrays[6].shape, F32),
        decay_log=vmem(arrays[7].shape, F32),
        skip_gain=vmem(arrays[8].shape, F32),
        out_gain=vmem(arrays[9].shape, F32),
        state_w=vmem((2, state_weight.shape[0], width), BF16),
        small=vmem((2, 8, LANES), F32),
        packf=vmem((n, EDGE, LANES), F32),
        pack=vmem((n, EDGE, LANES), BF16),
        edge1=vmem((sources, EDGE, LANES), BF16),
        edge2=vmem((edge, width), BF16),
        edge_u=vmem((EDGE, width), F32),
        r1=vmem((full, block, width), BF16),
        o1=vmem((full, block, width), BF16),
        r2=vmem((rows, cols, width), BF16),
        x0=vmem((full + taps - 1, block, inner), F32),
        p0=vmem((full + taps - 1, block, LANES), F32),
        z0=vmem((full, block, inner), F32),
        x1=vmem((inner // LANES, tokens + EDGE, LANES), F32),
        p1=vmem((tokens + EDGE, LANES), F32),
        z1=vmem((tokens, inner), F32),
        xc=vmem((tokens, inner), BF16),
        y0=vmem((tokens, inner), F32),
        y1=vmem((inner // LANES, tokens, LANES), F32),
        ent1=vmem((2, tokens, LANES), F32),
        neg0=vmem((size0, size0), F32),
        neg1=vmem((size1, size1), F32),
        sum0=vmem((size0, size0), BF16),
        sum1=vmem((size1, size1), BF16),
        diag=vmem((HEADS * STATE, inner), BF16),
        local=vmem((groups, STATE, inner), F32),
        grown_last=vmem((SUB, inner), F32),
        sent=vmem((2, parts, STATE, 256 + LANES), BF16),
        gathered=vmem((2, n, parts, STATE, 256 + LANES), BF16),
        w_sem=dma((12,)),
        l_sem=dma((2 + chunks,)),
        s1=dma((n,)),
        v1=dma((n,)),
        e1s=dma((n,)),
        e1r=dma((sources,)),
        s2=dma((chunks, n)),
        v2=dma((chunks, n)),
        e2s=dma((n,)),
        e2r=dma,
        gs=dma((2, parts, n)),
        gr=dma((2, parts, n)),
    )
    names = list(operands) + ["out"] + list(scratch)
    return pl.pallas_call(
        functools.partial(kernel, n, names),
        out_shape=vmem((rows, cols, width), BF16),
        in_specs=[pl.BlockSpec(memory_space=pl.ANY)] * len(operands),
        out_specs=pl.BlockSpec(memory_space=vmem),
        scratch_shapes=list(scratch.values()),
        compiler_params=pltpu.CompilerParams(
            collective_id=0, has_side_effects=True, vmem_limit_bytes=56 * 1024 * 1024
        ),
    )(*operands.values())


def solution(mesh):
    placed = (P(("dp", "seq"), None, None),) + (P(),) * 10
    return jax.shard_map(
        functools.partial(on_device, mesh.shape["seq"]),
        mesh=mesh,
        in_specs=placed,
        out_specs=P(("dp", "seq"), None, None),
        check_vma=False,
    )
```

```python
import functools
import math

import jax
import jax.numpy as jnp
from jax import lax
from jax.experimental import pallas as pl
from jax.experimental.pallas import tpu as pltpu
from jax.sharding import PartitionSpec as P

HEADS = 12
HEADDIM = 64
STATE = 16
LANES = 128
SUB = 8
EDGE = 16
EPS = 1e-05
LOG2E = math.log2(math.e)
MESH = pl.DeviceIdType.MESH
F32 = jnp.float32
BF16 = jnp.bfloat16


def silu(v):
    half = 0.5 * v
    return half + half * jnp.tanh(half)


def rms(v, gain):
    return v * lax.rsqrt(jnp.mean(v * v, axis=-1, keepdims=True) + EPS) * gain


def iota(shape, dim):
    return lax.broadcasted_iota(jnp.int32, shape, dim)


def dot(a, b):
    return jnp.dot(a, b, preferred_element_type=F32)


def dot_nt(a, b):
    return lax.dot_general(a, b, (((1,), (1,)), ((), ())), preferred_element_type=F32)


def xor(a, b, bits):
    total = 0
    for i in range(bits):
        total = total + lax.rem(a // 2**i + b // 2**i, 2) * 2**i
    return total


def kernel(n, names, *all_refs):
    r = dict(zip(names, all_refs))
    out = r["out"]
    slide, in_hbm, out_hbm = r["slide"], r["in_hbm"], r["out_hbm"]
    me = lax.axis_index("seq")
    rows, cols, width = slide.shape
    full = rows * n
    block = cols // n
    tokens = rows * cols
    inner = in_hbm.shape[2] // 2
    taps = r["conv_weight_hbm"].shape[1]
    proj = r["state_weight_hbm"].shape[0]
    bits = n.bit_length() - 1
    chips = n // 2
    chip = me // 2
    sources = -(-(taps - 1) // rows)
    pieces = width // LANES
    edge = min(EDGE, block)
    ocols = min(16, block)
    chunks = block // ocols
    size0 = full * SUB
    size1 = min(LANES, cols)
    lines1 = size1 // SUB
    part = 256
    parts = inner // part

    def remote(src, dst, send_sem, recv_sem, to):
        return pltpu.make_async_remote_copy(
            src_ref=src,
            dst_ref=dst,
            send_sem=send_sem,
            recv_sem=recv_sem,
            device_id={"seq": to},
            device_id_type=MESH,
        )

    barrier = pltpu.get_barrier_semaphore()
    for k in range(1, n):
        pl.semaphore_signal(
            barrier, inc=1, device_id={"seq": lax.rem(me + k, n)}, device_id_type=MESH
        )

    w_sem = r["w_sem"]
    local_in = [pltpu.make_async_copy(slide, r["slide_v"], w_sem.at[0])]
    small_names = [name[:-4] for name in names if name.endswith("_hbm") and name[:-4] in names]
    small_names = [name for name in small_names if name not in ("in", "out")]
    smalls = [
        pltpu.make_async_copy(r[name + "_hbm"], r[name], w_sem.at[1 + i])
        for i, name in enumerate(small_names)
    ]
    base = 1 + len(small_names)
    weights = [
        pltpu.make_async_copy(in_hbm.at[0], r["in_w"].at[0], w_sem.at[base]),
        pltpu.make_async_copy(in_hbm.at[1], r["in_w"].at[1], w_sem.at[base + 1]),
        pltpu.make_async_copy(out_hbm, r["out_w"], w_sem.at[base + 2]),
    ]
    local_in[0].start()
    for copy in smalls:
        copy.start()
    weights[0].start()
    weights[2].start()
    weights[1].start()

    norm_gain, conv_weight, conv_bias = r["norm_gain"], r["conv_weight"], r["conv_bias"]
    in_w, out_w, out_gain = r["in_w"], r["out_w"], r["out_gain"]
    slide_v, r1, r2, o1 = r["slide_v"], r["r1"], r["r2"], r["o1"]
    edge1, edge2, pack = r["edge1"], r["edge2"], r["pack"]

    def at_cols(j):
        return pl.ds(pl.multiple_of(j * block, block), block)

    def at_rows(j):
        return pl.ds(j * rows, rows)

    local_in[0].wait()
    packf = r["packf"]
    packf[...] = jnp.zeros_like(packf)
    for j in range(n - 1):
        for i in range(rows):
            at = (j + 1) * block
            line = slide_v[i, at : at + SUB, :].astype(F32)
            for q in range(pieces):
                packf[j, i * pieces + q : i * pieces + q + 1, :] = line[
                    0:1, q * LANES : (q + 1) * LANES
                ]
    pack[...] = packf[...].astype(BF16)

    r["gathered"][...] = jnp.zeros_like(r["gathered"])
    pl.semaphore_wait(barrier, n - 1)

    def first_copy(mask):
        to = xor(me, mask, bits)
        return remote(
            slide_v.at[:, at_cols(to), :],
            r1.at[at_rows(me)],
            r["s1"].at[mask],
            r["v1"].at[mask],
            to,
        )

    for mask in range(1, n):
        first_copy(mask).start()

    def edge1_copy(source, j):
        return remote(
            pack.at[j],
            edge1.at[source],
            r["e1s"].at[j],
            r["e1r"].at[source],
            j,
        )

    for source in range(sources):

        @pl.when(me == source)
        def _():
            for j in range(n - 1):
                if j != source:
                    edge1_copy(source, j).start()
            edge1[source] = pack[source]

    own = pltpu.make_async_copy(slide_v.at[:, at_cols(me), :], r1.at[at_rows(me)], r["l_sem"].at[0])
    own.start()

    @pl.when(me == n - 1)
    def _():
        edge1[...] = jnp.zeros_like(edge1)

    @pl.when(me == 0)
    def _():
        edge2[...] = jnp.zeros_like(edge2)

    head_mask = iota((STATE, inner), 0) == iota((STATE, inner), 1) // HEADDIM

    def spread(column):
        return jnp.sum(jnp.where(head_mask, column, 0.0), axis=0, keepdims=True)

    diag = r["diag"]
    diag[...] = jnp.where(
        iota((HEADS * STATE, inner), 0) // STATE == iota((HEADS * STATE, inner), 1) // HEADDIM,
        1.0,
        0.0,
    ).astype(BF16)

    def key(v, lines):
        return lax.rem(v, SUB) * lines + v // SUB

    order0 = [key(iota((size0, size0), i), full) for i in range(2)]
    order1 = [key(iota((size1, size1), i), lines1) for i in range(2)]
    r["neg0"][...] = jnp.where(order0[1] >= order0[0], 0.0, -jnp.inf)
    r["sum0"][...] = jnp.where(order0[0] >= order0[1], 1.0, 0.0).astype(BF16)
    r["neg1"][...] = jnp.where(order1[1] <= order1[0], 0.0, -jnp.inf)
    r["sum1"][...] = jnp.where(order1[0] <= order1[1], 1.0, 0.0).astype(BF16)

    small = r["small"]
    small[...] = jnp.zeros_like(small)
    p0, p1 = r["p0"], r["p1"]
    p0[...] = jnp.zeros_like(p0)
    p1[...] = jnp.zeros_like(p1)
    edge_u = r["edge_u"]
    edge_u[...] = jnp.zeros_like(edge_u)
    for copy in smalls:
        copy.wait()
    columns = []
    for layer in range(2):
        small[layer, 0:taps, 0 : 2 * STATE] = conv_weight[layer, :, inner : inner + 2 * STATE]
        small[layer, 4:5, 0 : 2 * STATE] = conv_bias[layer : layer + 1, inner : inner + 2 * STATE]
        small[layer, 5:6, 0:HEADS] = r["step_bias"][layer : layer + 1, :]
        small[layer, 6:7, 0:HEADS] = r["decay_log"][layer : layer + 1, :]
        small[layer, 7:8, 0:HEADS] = r["skip_gain"][layer : layer + 1, :]
        r["state_w"][layer] = r["state_weight"][:, layer, :]
        turned = jnp.transpose(small[layer])
        columns.append([turned[0:STATE, 5 + i : 6 + i] for i in range(3)])

    def project(layer, u):
        normed = rms(u.astype(F32), norm_gain[layer : layer + 1, :]).astype(BF16)
        p = dot_nt(normed, r["state_w"][layer]).astype(BF16).astype(F32)
        x = dot(normed, in_w[layer, :, inner:]).astype(BF16).astype(F32)
        return normed, x, p

    def gate(layer, normed):
        return silu(dot(normed, in_w[layer, :, :inner]).astype(BF16).astype(F32))

    xc_ref, y0, y1, ent1 = r["xc"], r["y0"], r["y1"], r["ent1"]

    def state_copy(layer, i, source, to):
        wide = part + LANES if i == 0 else part
        return remote(
            r["sent"].at[layer, i, :, 0:wide],
            r["gathered"].at[layer, source, i, :, 0:wide],
            r["gs"].at[layer, i, to],
            r["gr"].at[layer, i, source],
            to,
        )

    def targets(backward):
        return range(0, n - 1) if backward else range(n - 1, 0, -1)

    def later(i, j, backward):
        return (i > j) if backward else (i < j)

    def before(layer, backward, groups, size, load_p, load_x, sum_ref):
        bias, decay_col, _ = columns[layer]
        rate_scale = -jnp.exp(decay_col) * LOG2E
        last_at = 0 if backward else size - 1
        sequence = list(range(groups))[:: -1 if backward else 1]
        turned, c_side = {}, {}
        lane = iota((size, LANES), 1)
        for g in sequence:
            windows = load_p(g)
            total = small[layer, 4:5, :] + small[layer, 0:1, :] * windows[0]
            for k in range(1, taps):
                total = total + small[layer, k : k + 1, :] * windows[k]
            bc = silu(total).astype(BF16).astype(F32)
            turned[g] = jnp.transpose(jnp.where(lane < 2 * STATE, bc, windows[-1]))
            c_side[g] = jnp.where((lane >= STATE) & (lane < 2 * STATE), bc, 0.0).astype(BF16)
        raw = bias + jnp.concatenate(
            [turned[g][2 * STATE : 3 * STATE] for g in sequence], axis=1
        )
        step = jnp.maximum(raw, 0.0) + jnp.log1p(jnp.exp(-jnp.abs(raw)))
        rate = step * rate_scale
        high = rate.astype(BF16)
        low = (rate - high.astype(F32)).astype(BF16)
        split = jnp.concatenate([high, low], axis=0)
        log_step = jnp.log2(step)
        total_last, kept, weighted, grown_last = None, {}, {}, {}
        for i, g in enumerate(sequence):
            at = slice(i * size, (i + 1) * size)
            both = dot(split[:, at], sum_ref[...])
            cum = both[0:STATE] + both[STATE : 2 * STATE]
            less = cum - log_step[:, at]
            last = cum[:, last_at : last_at + 1]
            tail = jnp.exp2(last - less)
            b_rows = turned[g][0:STATE]
            weighted[g] = jnp.concatenate(
                [b_rows * tail[h : h + 1, :] for h in range(HEADS)], axis=0
            ).astype(BF16)
            grown_last[g] = spread(jnp.exp2(last))
            r["grown_last"][g : g + 1, :] = grown_last[g]
            total_last = last if total_last is None else total_last + last
            kept[g] = (turned[g], c_side[g], cum, less)
        decay = jnp.exp2(total_last)
        decay_high = decay.astype(BF16).astype(F32)
        lane = iota((STATE, LANES), 1)
        sent = r["sent"]
        sent[layer, 0, :, part : part + LANES] = jnp.where(
            lane == 0, decay_high, jnp.where(lane == 1, decay - decay_high, 0.0)
        ).astype(BF16)
        heads_per = part // HEADDIM
        lane = iota((STATE, part), 1) // HEADDIM
        for i in range(parts):
            whole = slice(i * part, (i + 1) * part)
            carried = None
            for g in sequence:
                here = slice(g * size, (g + 1) * size)
                for q in range(i * part // LANES, (i + 1) * part // LANES):
                    at = slice(q * LANES, (q + 1) * LANES)
                    windows = load_x(g, q)
                    low = [w.astype(BF16) for w in windows]
                    total = conv_bias[layer : layer + 1, at].astype(BF16) + (
                        conv_weight[layer, 0:1, at].astype(BF16) * low[0]
                    )
                    for k in range(1, taps):
                        total = total + conv_weight[layer, k : k + 1, at].astype(BF16) * low[k]
                    xc_ref[here, at] = silu(total)
                got = dot(
                    weighted[g][i * heads_per * STATE : (i + 1) * heads_per * STATE],
                    xc_ref[here, whole],
                )
                local = got[0:STATE]
                for h in range(1, heads_per):
                    local = jnp.where(lane == h, got[h * STATE : (h + 1) * STATE], local)
                r["local"][g, :, whole] = local
                carried = local if carried is None else grown_last[g][:, whole] * carried + local
            sent[layer, i, :, 0:part] = carried.astype(BF16)
            for to in targets(backward):

                @pl.when(later(me, to, backward))
                def _():
                    state_copy(layer, i, me, to).start()

        return sequence, kept

    def within(layer, sequence, kept, size, neg_ref):
        skip = spread(columns[layer][2])
        even = iota((size, LANES), 1) < HEADDIM
        entering = {}
        for g in sequence:
            here = slice(g * size, (g + 1) * size)
            turned, c_side, cum, less = kept[g]
            b_rows, c_rows = turned[0:STATE], turned[STATE : 2 * STATE]
            both_b = [b_rows, b_rows, jnp.zeros((LANES - 2 * STATE, size), F32)]
            scores = dot(c_side, jnp.concatenate(both_b, axis=0).astype(BF16))
            grown = jnp.exp2(cum)
            stack = [c_rows * grown[h : h + 1, :] for h in range(HEADS)] + [cum]
            stack.append(jnp.zeros((-STATE * (HEADS + 1) % LANES, size), F32))
            across = jnp.transpose(jnp.concatenate(stack, axis=0))
            if layer == 0:
                entering[g] = across[:, 0 : HEADS * STATE].astype(BF16)
            else:
                for q in range(2):
                    for i in range(lines1):
                        ent1[q, pl.ds(g * size + i, SUB, stride=lines1), :] = across[
                            i * SUB : (i + 1) * SUB, q * LANES : (q + 1) * LANES
                        ]
            for pair in range(HEADS // 2):
                at = slice(pair * LANES, (pair + 1) * LANES)
                xp = xc_ref[here, at]
                weights = []
                for h in (2 * pair, 2 * pair + 1):
                    column = across[:, HEADS * STATE + h : HEADS * STATE + h + 1]
                    diff = (column - less[h : h + 1, :]) + neg_ref[...]
                    weights.append((scores * jnp.exp2(diff)).astype(BF16))
                zero = jnp.zeros_like(xp)
                stacked = jnp.concatenate(
                    [jnp.where(even, xp, zero), jnp.where(even, zero, xp)], axis=0
                )
                y = skip[:, at] * xp.astype(F32) + dot(jnp.concatenate(weights, axis=1), stacked)
                if layer == 0:
                    y0[here, at] = y
                else:
                    for i in range(lines1):
                        y1[pair, pl.ds(g * size + i, SUB, stride=lines1), :] = y[
                            i * SUB : (i + 1) * SUB
                        ]
        if layer == 1:
            for g in sequence:
                here = slice(g * size, (g + 1) * size)
                entering[g] = jnp.concatenate(
                    [ent1[0, here, :], ent1[1, here, 0 : HEADS * STATE - LANES]], axis=1
                ).astype(BF16)
        return entering

    def arrived(layer, backward):
        gathered = r["gathered"]
        factors, state = {}, []
        order = range(n - 1, 0, -1) if backward else range(0, n - 1)
        for i in range(parts):
            whole = slice(i * part, (i + 1) * part)
            for source in order:

                @pl.when(later(source, me, backward))
                def _():
                    state_copy(layer, i, source, (source + 1) % n).wait_recv()

            total = jnp.zeros((STATE, part), F32)
            for source in order:
                valid = later(source, me, backward)
                if i == 0:
                    packed = gathered[layer, source, 0, :, part : part + LANES].astype(F32)
                    factor = spread(jnp.sum(packed, axis=1, keepdims=True))
                    factors[source] = jnp.where(valid, factor, 1.0)
                came = gathered[layer, source, i, :, 0:part].astype(F32)
                total = factors[source][:, whole] * total + jnp.where(valid, came, 0.0)
            state.append(total)
        return jnp.concatenate(state, axis=1)

    def step_out(g, entering, state):
        low = state.astype(BF16)
        wide = jnp.concatenate([low] * HEADS, axis=0) * diag[...]
        inter = dot(entering[g], wide)
        return inter, r["grown_last"][g : g + 1, :] * state + r["local"][g]

    def finish(layer, y, sz, token):
        gated = y * sz
        scale = lax.rsqrt(jnp.mean(gated * gated, axis=-1, keepdims=True) + EPS)
        mixed = (gated * out_gain[layer : layer + 1, :]).astype(BF16)
        return (token.astype(F32) + scale * dot(mixed, out_w[layer])).astype(BF16)

    x0, z0 = r["x0"], r["z0"]
    weights[0].wait()
    last_normed = None
    for k in range(chips):
        source = xor(chip, k, bits - 1)
        if k == 0:
            own.wait()
            first_copy(1).wait_recv()
        else:
            first_copy(2 * k).wait_recv()
            first_copy(2 * k + 1).wait_recv()
        if k == chips - 1:
            for i in range(sources):

                @pl.when((me != i) & (me < n - 1))
                def _():
                    edge1_copy(i, 0 if i else 1).wait_recv()

            for i in range(taps - 1):
                line = edge1[i // rows].astype(F32)
                for q in range(pieces):
                    j = (i % rows) * pieces + q
                    edge_u[i : i + 1, q * LANES : (q + 1) * LANES] = line[j : j + 1, :]
        at = pl.ds(source * 2 * rows, 2 * rows)
        count = 2 * rows * block
        u = r1[at].reshape(count, width)
        if k == chips - 1:
            u = jnp.concatenate([u, edge_u[...].astype(BF16)], axis=0)
        normed, x, p = project(0, u)
        p0[at, :, 0:proj] = p[0:count].reshape(2 * rows, block, proj)
        x0[at] = x[0:count].reshape(2 * rows, block, inner)
        if k < chips - 1:
            z0[at] = gate(0, normed).reshape(2 * rows, block, inner)
        else:
            last_normed, last_at = normed[0:count], at
            edge_x = x[count:]
            edge_p = jnp.concatenate(
                [p[count:], jnp.zeros((EDGE, LANES - proj), F32)], axis=1
            )
    for i in range(taps - 1):
        for ref, line in ((p0, edge_p), (x0, edge_x)):
            wide = ref.shape[2]
            moved = pltpu.roll(ref[i], block - 1, 0)
            final = iota((block, wide), 0) == block - 1
            ref[full + i] = jnp.where(final, line[i : i + 1, :], moved)

    groups0 = block // SUB

    def windows0(ref, g, at):
        first = [taps - 1 - k for k in range(taps)]
        at_g = slice(g * SUB, (g + 1) * SUB)
        return [ref[i : i + full, at_g, at].reshape(size0, LANES) for i in first]

    sequence, kept = before(
        0,
        True,
        groups0,
        size0,
        lambda g: windows0(p0, g, slice(0, LANES)),
        lambda g, q: windows0(x0, g, slice(q * LANES, (q + 1) * LANES)),
        r["sum0"],
    )
    z0[last_at] = gate(0, last_normed).reshape(2 * rows, block, inner)
    entering = within(0, sequence, kept, size0, r["neg0"])
    state = arrived(0, True)
    weights[2].wait()

    def second_copy(chunk, mask):
        to = xor(me, mask, bits)
        return remote(
            o1.at[at_rows(to), chunk * ocols : (chunk + 1) * ocols, :],
            r2.at[:, pl.ds(pl.multiple_of(me * block + chunk * ocols, ocols), ocols), :],
            r["s2"].at[chunk, mask],
            r["v2"].at[chunk, mask],
            to,
        )

    def own2_copy(chunk):
        return pltpu.make_async_copy(
            o1.at[at_rows(me), chunk * ocols : (chunk + 1) * ocols, :],
            r2.at[:, pl.ds(pl.multiple_of(me * block + chunk * ocols, ocols), ocols), :],
            r["l_sem"].at[1 + chunk],
        )

    def edge2_copy(j):
        return remote(
            o1.at[rows * j - 1, pl.ds(block - edge, edge), :],
            edge2,
            r["e2s"].at[j],
            r["e2r"],
            j,
        )

    edge2_own = pltpu.make_async_copy(
        o1.at[rows * (n - 1) - 1, pl.ds(block - edge, edge), :], edge2, r["l_sem"].at[1 + chunks]
    )

    for chunk in reversed(range(chunks)):
        ys = []
        for g in reversed(range(chunk * ocols // SUB, (chunk + 1) * ocols // SUB)):
            inter, state = step_out(g, entering, state)
            y = y0[g * size0 : (g + 1) * size0, :] + inter
            ys.insert(0, y.reshape(full, SUB, inner))
        at = slice(chunk * ocols, (chunk + 1) * ocols)
        flat = full * ocols
        y = jnp.concatenate(ys, axis=1).reshape(flat, inner)
        after = finish(0, y, z0[:, at, :].reshape(flat, inner), r1[:, at, :].reshape(flat, width))
        o1[:, at, :] = after.reshape(full, ocols, width)
        for mask in range(1, n):
            second_copy(chunk, mask).start()
        own2_copy(chunk).start()
        if chunk == chunks - 1:

            @pl.when(me == n - 1)
            def _():
                for j in range(1, n - 1):
                    edge2_copy(j).start()
                edge2_own.start()

    x1, z1 = r["x1"], r["z1"]
    weights[1].wait()
    pair = 2 * block
    for k in range(chips):
        source = xor(chip, k, bits - 1)
        for chunk in reversed(range(chunks)):
            if k == 0:
                own2_copy(chunk).wait()
                second_copy(chunk, 1).wait_recv()
            else:
                second_copy(chunk, 2 * k).wait_recv()
                second_copy(chunk, 2 * k + 1).wait_recv()
        at = pl.ds(pl.multiple_of(source * pair, pair), pair)
        count = rows * pair
        u = r2[:, at, :].reshape(count, width)
        if k == chips - 1:

            @pl.when((me > 0) & (me < n - 1))
            def _():
                edge2_copy(1).wait_recv()

            @pl.when(me == n - 1)
            def _():
                edge2_own.wait()

            edge_in = edge2[...]
            if edge < EDGE:
                edge_in = jnp.concatenate([jnp.zeros((EDGE - edge, width), BF16), edge_in], axis=0)
            u = jnp.concatenate([u, edge_in], axis=0)
        normed, x, p = project(1, u)

        def put(to_row, from_row):
            p1[to_row, 0:proj] = p[from_row]
            for q in range(inner // LANES):
                x1[q, to_row, :] = x[from_row, q * LANES : (q + 1) * LANES]

        for i in range(rows):
            to_row = pl.ds(pl.multiple_of(EDGE + i * cols + source * pair, SUB), pair)
            put(to_row, slice(i * pair, (i + 1) * pair))
        if k < chips - 1:
            sz = gate(1, normed)
            for i in range(rows):
                to_row = pl.ds(pl.multiple_of(i * cols + source * pair, SUB), pair)
                z1[to_row, :] = sz[i * pair : (i + 1) * pair]
        else:
            last_normed = normed[0:count]
            put(slice(0, EDGE), slice(count, count + EDGE))

    groups1 = tokens // size1

    def windows1(ref, g, lead):
        first = EDGE - (taps - 1) + g * size1
        lines = [
            ref[lead + (pl.ds(first + i, SUB, stride=lines1), slice(None))]
            for i in range(lines1 + taps - 1)
        ]
        return [jnp.concatenate(lines[k : k + lines1], axis=0) for k in range(taps)]

    sequence, kept = before(
        1,
        False,
        groups1,
        size1,
        lambda g: windows1(p1, g, ()),
        lambda g, q: windows1(x1, g, (q,)),
        r["sum1"],
    )
    sz = gate(1, last_normed)
    source = xor(chip, chips - 1, bits - 1)
    for i in range(rows):
        to_row = pl.ds(pl.multiple_of(i * cols + source * pair, SUB), pair)
        z1[to_row, :] = sz[i * pair : (i + 1) * pair]
    entering = within(1, sequence, kept, size1, r["neg1"])
    for mask in range(1, n):
        first_copy(mask).wait_send()
        for chunk in range(chunks):
            second_copy(chunk, mask).wait_send()
    for source in range(sources):

        @pl.when(me == source)
        def _():
            for j in range(n - 1):
                if j != source:
                    edge1_copy(source, j).wait_send()

    @pl.when(me == n - 1)
    def _():
        for j in range(1, n - 1):
            edge2_copy(j).wait_send()

    def states_sent(layer):
        for to in targets(layer == 0):

            @pl.when(later(me, to, layer == 0))
            def _():
                for i in range(parts):
                    state_copy(layer, i, me, to).wait_send()

    states_sent(0)
    state = arrived(1, False)
    per_row = groups1 // rows
    for i in range(rows):
        ys = []
        for g in range(i * per_row, (i + 1) * per_row):
            inter, state = step_out(g, entering, state)
            here = slice(g * size1, (g + 1) * size1)
            y = jnp.concatenate([y1[q, here, :] for q in range(inner // LANES)], axis=1)
            ys.append(y + inter)
        y = jnp.concatenate(ys, axis=0)
        out[i] = finish(1, y, z1[i * cols : (i + 1) * cols, :], r2[i])
    states_sent(1)


def on_device(n, *arrays):
    slide, in_weight, out_weight = arrays[0], arrays[2], arrays[10]
    rows, cols, width = slide.shape
    full, block, tokens = rows * n, cols // n, rows * cols
    inner = in_weight.shape[2] // 2
    edge = min(EDGE, block)
    taps = arrays[4].shape[1]
    sources = -(-(taps - 1) // rows)
    chunks = block // min(16, block)
    size0, size1 = full * SUB, min(LANES, cols)
    groups = max(tokens // size0, tokens // size1)
    parts = inner // 256
    state_weight = jnp.transpose(arrays[3], (2, 0, 1))
    operands = dict(
        slide=slide,
        norm_gain_hbm=arrays[1],
        in_hbm=in_weight,
        state_weight_hbm=state_weight,
        conv_weight_hbm=arrays[4],
        conv_bias_hbm=arrays[5],
        step_bias_hbm=arrays[6],
        decay_log_hbm=arrays[7],
        skip_gain_hbm=arrays[8],
        out_gain_hbm=arrays[9],
        out_hbm=out_weight,
    )
    dma = pltpu.SemaphoreType.DMA
    vmem = pltpu.VMEM
    scratch = dict(
        slide_v=vmem(slide.shape, BF16),
        in_w=vmem(in_weight.shape, BF16),
        out_w=vmem(out_weight.shape, BF16),
        norm_gain=vmem(arrays[1].shape, F32),
        state_weight=vmem(state_weight.shape, BF16),
        conv_weight=vmem(arrays[4].shape, F32),
        conv_bias=vmem(arrays[5].shape, F32),
        step_bias=vmem(arrays[6].shape, F32),
        decay_log=vmem(arrays[7].shape, F32),
        skip_gain=vmem(arrays[8].shape, F32),
        out_gain=vmem(arrays[9].shape, F32),
        state_w=vmem((2, state_weight.shape[0], width), BF16),
        small=vmem((2, 8, LANES), F32),
        packf=vmem((n, EDGE, LANES), F32),
        pack=vmem((n, EDGE, LANES), BF16),
        edge1=vmem((sources, EDGE, LANES), BF16),
        edge2=vmem((edge, width), BF16),
        edge_u=vmem((EDGE, width), F32),
        r1=vmem((full, block, width), BF16),
        o1=vmem((full, block, width), BF16),
        r2=vmem((rows, cols, width), BF16),
        x0=vmem((full + taps - 1, block, inner), F32),
        p0=vmem((full + taps - 1, block, LANES), F32),
        z0=vmem((full, block, inner), F32),
        x1=vmem((inner // LANES, tokens + EDGE, LANES), F32),
        p1=vmem((tokens + EDGE, LANES), F32),
        z1=vmem((tokens, inner), F32),
        xc=vmem((tokens, inner), BF16),
        y0=vmem((tokens, inner), F32),
        y1=vmem((inner // LANES, tokens, LANES), F32),
        ent1=vmem((2, tokens, LANES), F32),
        neg0=vmem((size0, size0), F32),
        neg1=vmem((size1, size1), F32),
        sum0=vmem((size0, size0), BF16),
        sum1=vmem((size1, size1), BF16),
        diag=vmem((HEADS * STATE, inner), BF16),
        local=vmem((groups, STATE, inner), F32),
        grown_last=vmem((SUB, inner), F32),
        sent=vmem((2, parts, STATE, 256 + LANES), BF16),
        gathered=vmem((2, n, parts, STATE, 256 + LANES), BF16),
        w_sem=dma((12,)),
        l_sem=dma((2 + chunks,)),
        s1=dma((n,)),
        v1=dma((n,)),
        e1s=dma((n,)),
        e1r=dma((sources,)),
        s2=dma((chunks, n)),
        v2=dma((chunks, n)),
        e2s=dma((n,)),
        e2r=dma,
        gs=dma((2, parts, n)),
        gr=dma((2, parts, n)),
    )
    names = list(operands) + ["out"] + list(scratch)
    return pl.pallas_call(
        functools.partial(kernel, n, names),
        out_shape=vmem((rows, cols, width), BF16),
        in_specs=[pl.BlockSpec(memory_space=pl.ANY)] * len(operands),
        out_specs=pl.BlockSpec(memory_space=vmem),
        scratch_shapes=list(scratch.values()),
        compiler_params=pltpu.CompilerParams(
            collective_id=0, has_side_effects=True, vmem_limit_bytes=56 * 1024 * 1024
        ),
    )(*operands.values())


def solution(mesh):
    placed = (P(("dp", "seq"), None, None),) + (P(),) * 10
    return jax.shard_map(
        functools.partial(on_device, mesh.shape["seq"]),
        mesh=mesh,
        in_specs=placed,
        out_specs=P(("dp", "seq"), None, None),
        check_vma=False,
    )
```

```python
import functools
import math

import jax
import jax.numpy as jnp
from jax import lax
from jax.experimental import pallas as pl
from jax.experimental.pallas import tpu as pltpu
from jax.sharding import PartitionSpec as P

HEADS = 12
HEADDIM = 64
STATE = 16
LANES = 128
SUB = 8
EDGE = 16
EPS = 1e-05
LOG2E = math.log2(math.e)
MESH = pl.DeviceIdType.MESH
F32 = jnp.float32
BF16 = jnp.bfloat16


def silu(v):
    half = 0.5 * v
    return half + half * jnp.tanh(half)


def rms(v, gain):
    return v * lax.rsqrt(jnp.mean(v * v, axis=-1, keepdims=True) + EPS) * gain


def iota(shape, dim):
    return lax.broadcasted_iota(jnp.int32, shape, dim)


def dot(a, b):
    return jnp.dot(a, b, preferred_element_type=F32)


def dot_nt(a, b):
    return lax.dot_general(a, b, (((1,), (1,)), ((), ())), preferred_element_type=F32)


def xor(a, b, bits):
    total = 0
    for i in range(bits):
        total = total + lax.rem(a // 2**i + b // 2**i, 2) * 2**i
    return total


def kernel(n, names, *all_refs):
    r = dict(zip(names, all_refs))
    out = r["out"]
    slide, in_hbm, out_hbm = r["slide"], r["in_hbm"], r["out_hbm"]
    me = lax.axis_index("seq")
    rows, cols, width = slide.shape
    full = rows * n
    block = cols // n
    tokens = rows * cols
    inner = in_hbm.shape[2] // 2
    taps = r["conv_weight_hbm"].shape[1]
    proj = r["state_weight_hbm"].shape[0]
    bits = n.bit_length() - 1
    chips = n // 2
    chip = me // 2
    sources = -(-(taps - 1) // rows)
    pieces = width // LANES
    edge = min(EDGE, block)
    ocols = min(16, block)
    chunks = block // ocols
    size0 = full * SUB
    size1 = min(LANES, cols)
    lines1 = size1 // SUB
    part = 256
    parts = inner // part

    def remote(src, dst, send_sem, recv_sem, to):
        return pltpu.make_async_remote_copy(
            src_ref=src,
            dst_ref=dst,
            send_sem=send_sem,
            recv_sem=recv_sem,
            device_id={"seq": to},
            device_id_type=MESH,
        )

    barrier = pltpu.get_barrier_semaphore()
    for k in range(1, n):
        pl.semaphore_signal(
            barrier, inc=1, device_id={"seq": lax.rem(me + k, n)}, device_id_type=MESH
        )

    w_sem = r["w_sem"]
    local_in = [pltpu.make_async_copy(slide, r["slide_v"], w_sem.at[0])]
    small_names = [name[:-4] for name in names if name.endswith("_hbm") and name[:-4] in names]
    small_names = [name for name in small_names if name not in ("in", "out")]
    smalls = [
        pltpu.make_async_copy(r[name + "_hbm"], r[name], w_sem.at[1 + i])
        for i, name in enumerate(small_names)
    ]
    base = 1 + len(small_names)
    weights = [
        pltpu.make_async_copy(in_hbm.at[0], r["in_w"].at[0], w_sem.at[base]),
        pltpu.make_async_copy(in_hbm.at[1], r["in_w"].at[1], w_sem.at[base + 1]),
        pltpu.make_async_copy(out_hbm, r["out_w"], w_sem.at[base + 2]),
    ]
    local_in[0].start()
    for copy in smalls:
        copy.start()
    weights[0].start()
    weights[2].start()
    weights[1].start()

    norm_gain, conv_weight, conv_bias = r["norm_gain"], r["conv_weight"], r["conv_bias"]
    in_w, out_w, out_gain = r["in_w"], r["out_w"], r["out_gain"]
    slide_v, r1, r2, o1 = r["slide_v"], r["r1"], r["r2"], r["o1"]
    edge1, edge2, pack = r["edge1"], r["edge2"], r["pack"]

    def at_cols(j):
        return pl.ds(pl.multiple_of(j * block, block), block)

    def at_rows(j):
        return pl.ds(j * rows, rows)

    local_in[0].wait()
    packf = r["packf"]
    packf[...] = jnp.zeros_like(packf)
    for j in range(n - 1):
        for i in range(rows):
            at = (j + 1) * block
            line = slide_v[i, at : at + SUB, :].astype(F32)
            for q in range(pieces):
                packf[j, i * pieces + q : i * pieces + q + 1, :] = line[
                    0:1, q * LANES : (q + 1) * LANES
                ]
    pack[...] = packf[...].astype(BF16)

    r["gathered"][...] = jnp.zeros_like(r["gathered"])
    pl.semaphore_wait(barrier, n - 1)

    def first_copy(mask):
        to = xor(me, mask, bits)
        return remote(
            slide_v.at[:, at_cols(to), :],
            r1.at[at_rows(me)],
            r["s1"].at[mask],
            r["v1"].at[mask],
            to,
        )

    for mask in range(1, n):
        first_copy(mask).start()

    def edge1_copy(source, j):
        return remote(
            pack.at[j],
            edge1.at[source],
            r["e1s"].at[j],
            r["e1r"].at[source],
            j,
        )

    for source in range(sources):

        @pl.when(me == source)
        def _():
            for j in range(n - 1):
                if j != source:
                    edge1_copy(source, j).start()
            edge1[source] = pack[source]

    own = pltpu.make_async_copy(slide_v.at[:, at_cols(me), :], r1.at[at_rows(me)], r["l_sem"].at[0])
    own.start()

    @pl.when(me == n - 1)
    def _():
        edge1[...] = jnp.zeros_like(edge1)

    @pl.when(me == 0)
    def _():
        edge2[...] = jnp.zeros_like(edge2)

    head_mask = iota((STATE, inner), 0) == iota((STATE, inner), 1) // HEADDIM

    def spread(column):
        return jnp.sum(jnp.where(head_mask, column, 0.0), axis=0, keepdims=True)

    diag = r["diag"]
    diag[...] = jnp.where(
        iota((HEADS * STATE, inner), 0) // STATE == iota((HEADS * STATE, inner), 1) // HEADDIM,
        1.0,
        0.0,
    ).astype(BF16)

    def key(v, lines):
        return lax.rem(v, SUB) * lines + v // SUB

    order0 = [key(iota((size0, size0), i), full) for i in range(2)]
    order1 = [key(iota((size1, size1), i), lines1) for i in range(2)]
    r["neg0"][...] = jnp.where(order0[1] >= order0[0], 0.0, -jnp.inf)
    r["sum0"][...] = jnp.where(order0[0] >= order0[1], 1.0, 0.0).astype(BF16)
    r["neg1"][...] = jnp.where(order1[1] <= order1[0], 0.0, -jnp.inf)
    r["sum1"][...] = jnp.where(order1[0] <= order1[1], 1.0, 0.0).astype(BF16)

    small = r["small"]
    small[...] = jnp.zeros_like(small)
    p0, p1 = r["p0"], r["p1"]
    p0[...] = jnp.zeros_like(p0)
    p1[...] = jnp.zeros_like(p1)
    edge_u = r["edge_u"]
    edge_u[...] = jnp.zeros_like(edge_u)
    for copy in smalls:
        copy.wait()
    columns = []
    for layer in range(2):
        small[layer, 0:taps, 0 : 2 * STATE] = conv_weight[layer, :, inner : inner + 2 * STATE]
        small[layer, 4:5, 0 : 2 * STATE] = conv_bias[layer : layer + 1, inner : inner + 2 * STATE]
        small[layer, 5:6, 0:HEADS] = r["step_bias"][layer : layer + 1, :]
        small[layer, 6:7, 0:HEADS] = r["decay_log"][layer : layer + 1, :]
        small[layer, 7:8, 0:HEADS] = r["skip_gain"][layer : layer + 1, :]
        r["state_w"][layer] = r["state_weight"][:, layer, :]
        turned = jnp.transpose(small[layer])
        columns.append([turned[0:STATE, 5 + i : 6 + i] for i in range(3)])

    def project(layer, u):
        normed = rms(u.astype(F32), norm_gain[layer : layer + 1, :]).astype(BF16)
        p = dot_nt(normed, r["state_w"][layer]).astype(BF16).astype(F32)
        x = dot(normed, in_w[layer, :, inner:]).astype(BF16).astype(F32)
        return normed, x, p

    def gate(layer, normed):
        return silu(dot(normed, in_w[layer, :, :inner]).astype(BF16).astype(F32))

    xc_ref, y0, y1, ent1 = r["xc"], r["y0"], r["y1"], r["ent1"]

    def state_copy(layer, i, source, to):
        wide = part + LANES if i == 0 else part
        return remote(
            r["sent"].at[layer, i, :, 0:wide],
            r["gathered"].at[layer, source, i, :, 0:wide],
            r["gs"].at[layer, i, to],
            r["gr"].at[layer, i, source],
            to,
        )

    def targets(backward):
        return range(0, n - 1) if backward else range(n - 1, 0, -1)

    def later(i, j, backward):
        return (i > j) if backward else (i < j)

    def before(layer, backward, groups, size, load_p, load_x, sum_ref):
        bias, decay_col, _ = columns[layer]
        rate_scale = -jnp.exp(decay_col) * LOG2E
        last_at = 0 if backward else size - 1
        sequence = list(range(groups))[:: -1 if backward else 1]
        turned, c_side = {}, {}
        lane = iota((size, LANES), 1)
        for g in sequence:
            windows = load_p(g)
            total = small[layer, 4:5, :] + small[layer, 0:1, :] * windows[0]
            for k in range(1, taps):
                total = total + small[layer, k : k + 1, :] * windows[k]
            bc = silu(total).astype(BF16).astype(F32)
            turned[g] = jnp.transpose(jnp.where(lane < 2 * STATE, bc, windows[-1]))
            c_side[g] = jnp.where((lane >= STATE) & (lane < 2 * STATE), bc, 0.0).astype(BF16)
        raw = bias + jnp.concatenate(
            [turned[g][2 * STATE : 3 * STATE] for g in sequence], axis=1
        )
        step = jnp.maximum(raw, 0.0) + jnp.log1p(jnp.exp(-jnp.abs(raw)))
        rate = step * rate_scale
        high = rate.astype(BF16)
        low = (rate - high.astype(F32)).astype(BF16)
        split = jnp.concatenate([high, low], axis=0)
        log_step = jnp.log2(step)
        total_last, kept, weighted, grown_last = None, {}, {}, {}
        for i, g in enumerate(sequence):
            at = slice(i * size, (i + 1) * size)
            both = dot(split[:, at], sum_ref[...])
            cum = both[0:STATE] + both[STATE : 2 * STATE]
            less = cum - log_step[:, at]
            last = cum[:, last_at : last_at + 1]
            tail = jnp.exp2(last - less)
            b_rows = turned[g][0:STATE]
            weighted[g] = jnp.concatenate(
                [b_rows * tail[h : h + 1, :] for h in range(HEADS)], axis=0
            ).astype(BF16)
            grown_last[g] = spread(jnp.exp2(last))
            r["grown_last"][g : g + 1, :] = grown_last[g]
            total_last = last if total_last is None else total_last + last
            kept[g] = (turned[g], c_side[g], cum, less)
        decay = jnp.exp2(total_last)
        decay_high = decay.astype(BF16).astype(F32)
        lane = iota((STATE, LANES), 1)
        sent = r["sent"]
        sent[layer, 0, :, part : part + LANES] = jnp.where(
            lane == 0, decay_high, jnp.where(lane == 1, decay - decay_high, 0.0)
        ).astype(BF16)
        heads_per = part // HEADDIM
        lane = iota((STATE, part), 1) // HEADDIM
        for i in range(parts):
            whole = slice(i * part, (i + 1) * part)
            carried = None
            for g in sequence:
                here = slice(g * size, (g + 1) * size)
                for q in range(i * part // LANES, (i + 1) * part // LANES):
                    at = slice(q * LANES, (q + 1) * LANES)
                    windows = load_x(g, q)
                    low = [w.astype(BF16) for w in windows]
                    total = conv_bias[layer : layer + 1, at].astype(BF16) + (
                        conv_weight[layer, 0:1, at].astype(BF16) * low[0]
                    )
                    for k in range(1, taps):
                        total = total + conv_weight[layer, k : k + 1, at].astype(BF16) * low[k]
                    xc_ref[here, at] = silu(total)
                got = dot(
                    weighted[g][i * heads_per * STATE : (i + 1) * heads_per * STATE],
                    xc_ref[here, whole],
                )
                local = got[0:STATE]
                for h in range(1, heads_per):
                    local = jnp.where(lane == h, got[h * STATE : (h + 1) * STATE], local)
                r["local"][g, :, whole] = local
                carried = local if carried is None else grown_last[g][:, whole] * carried + local
            sent[layer, i, :, 0:part] = carried.astype(BF16)
            for to in targets(backward):

                @pl.when(later(me, to, backward))
                def _():
                    state_copy(layer, i, me, to).start()

        return sequence, kept

    def within(layer, sequence, kept, size, neg_ref):
        skip = spread(columns[layer][2])
        even = iota((size, LANES), 1) < HEADDIM
        entering = {}
        for g in sequence:
            here = slice(g * size, (g + 1) * size)
            turned, c_side, cum, less = kept[g]
            b_rows, c_rows = turned[0:STATE], turned[STATE : 2 * STATE]
            both_b = [b_rows, b_rows, jnp.zeros((LANES - 2 * STATE, size), F32)]
            scores = dot(c_side, jnp.concatenate(both_b, axis=0).astype(BF16))
            scores = jnp.where(neg_ref[...] == 0.0, scores, 0.0)
            most = cum - less
            grown = jnp.exp2(cum)
            stack = [c_rows * grown[h : h + 1, :] for h in range(HEADS)] + [cum]
            stack.append(jnp.zeros((-STATE * (HEADS + 1) % LANES, size), F32))
            across = jnp.transpose(jnp.concatenate(stack, axis=0))
            if layer == 0:
                entering[g] = across[:, 0 : HEADS * STATE].astype(BF16)
            else:
                for q in range(2):
                    for i in range(lines1):
                        ent1[q, pl.ds(g * size + i, SUB, stride=lines1), :] = across[
                            i * SUB : (i + 1) * SUB, q * LANES : (q + 1) * LANES
                        ]
            for pair in range(HEADS // 2):
                at = slice(pair * LANES, (pair + 1) * LANES)
                xp = xc_ref[here, at]
                weights = []
                for h in (2 * pair, 2 * pair + 1):
                    column = across[:, HEADS * STATE + h : HEADS * STATE + h + 1]
                    diff = jnp.minimum(column - less[h : h + 1, :], most[h : h + 1, :])
                    weights.append((scores * jnp.exp2(diff)).astype(BF16))
                zero = jnp.zeros_like(xp)
                stacked = jnp.concatenate(
                    [jnp.where(even, xp, zero), jnp.where(even, zero, xp)], axis=0
                )
                y = skip[:, at] * xp.astype(F32) + dot(jnp.concatenate(weights, axis=1), stacked)
                if layer == 0:
                    y0[here, at] = y
                else:
                    for i in range(lines1):
                        y1[pair, pl.ds(g * size + i, SUB, stride=lines1), :] = y[
                            i * SUB : (i + 1) * SUB
                        ]
        if layer == 1:
            for g in sequence:
                here = slice(g * size, (g + 1) * size)
                entering[g] = jnp.concatenate(
                    [ent1[0, here, :], ent1[1, here, 0 : HEADS * STATE - LANES]], axis=1
                ).astype(BF16)
        return entering

    def arrived(layer, backward):
        gathered = r["gathered"]
        factors, state = {}, []
        order = range(n - 1, 0, -1) if backward else range(0, n - 1)
        for i in range(parts):
            whole = slice(i * part, (i + 1) * part)
            for source in order:

                @pl.when(later(source, me, backward))
                def _():
                    state_copy(layer, i, source, (source + 1) % n).wait_recv()

            total = jnp.zeros((STATE, part), F32)
            for source in order:
                valid = later(source, me, backward)
                if i == 0:
                    packed = gathered[layer, source, 0, :, part : part + LANES].astype(F32)
                    factor = spread(jnp.sum(packed, axis=1, keepdims=True))
                    factors[source] = jnp.where(valid, factor, 1.0)
                came = gathered[layer, source, i, :, 0:part].astype(F32)
                total = factors[source][:, whole] * total + jnp.where(valid, came, 0.0)
            state.append(total)
        return jnp.concatenate(state, axis=1)

    def step_out(g, entering, state):
        low = state.astype(BF16)
        wide = jnp.concatenate([low] * HEADS, axis=0) * diag[...]
        inter = dot(entering[g], wide)
        return inter, r["grown_last"][g : g + 1, :] * state + r["local"][g]

    def finish(layer, y, sz, token):
        gated = y * sz
        scale = lax.rsqrt(jnp.mean(gated * gated, axis=-1, keepdims=True) + EPS)
        mixed = (gated * out_gain[layer : layer + 1, :]).astype(BF16)
        return (token.astype(F32) + scale * dot(mixed, out_w[layer])).astype(BF16)

    x0, z0 = r["x0"], r["z0"]
    weights[0].wait()
    last_normed = None
    for k in range(chips):
        source = xor(chip, k, bits - 1)
        if k == 0:
            own.wait()
            first_copy(1).wait_recv()
        else:
            first_copy(2 * k).wait_recv()
            first_copy(2 * k + 1).wait_recv()
        if k == chips - 1:
            for i in range(sources):

                @pl.when((me != i) & (me < n - 1))
                def _():
                    edge1_copy(i, 0 if i else 1).wait_recv()

            for i in range(taps - 1):
                line = edge1[i // rows].astype(F32)
                for q in range(pieces):
                    j = (i % rows) * pieces + q
                    edge_u[i : i + 1, q * LANES : (q + 1) * LANES] = line[j : j + 1, :]
        at = pl.ds(source * 2 * rows, 2 * rows)
        count = 2 * rows * block
        u = r1[at].reshape(count, width)
        if k == chips - 1:
            u = jnp.concatenate([u, edge_u[...].astype(BF16)], axis=0)
        normed, x, p = project(0, u)
        p0[at, :, 0:proj] = p[0:count].reshape(2 * rows, block, proj)
        x0[at] = x[0:count].reshape(2 * rows, block, inner)
        if k < chips - 1:
            z0[at] = gate(0, normed).reshape(2 * rows, block, inner)
        else:
            last_normed, last_at = normed[0:count], at
            edge_x = x[count:]
            edge_p = jnp.concatenate(
                [p[count:], jnp.zeros((EDGE, LANES - proj), F32)], axis=1
            )
    for i in range(taps - 1):
        for ref, line in ((p0, edge_p), (x0, edge_x)):
            wide = ref.shape[2]
            moved = pltpu.roll(ref[i], block - 1, 0)
            final = iota((block, wide), 0) == block - 1
            ref[full + i] = jnp.where(final, line[i : i + 1, :], moved)

    groups0 = block // SUB

    def windows0(ref, g, at):
        first = [taps - 1 - k for k in range(taps)]
        at_g = slice(g * SUB, (g + 1) * SUB)
        return [ref[i : i + full, at_g, at].reshape(size0, LANES) for i in first]

    sequence, kept = before(
        0,
        True,
        groups0,
        size0,
        lambda g: windows0(p0, g, slice(0, LANES)),
        lambda g, q: windows0(x0, g, slice(q * LANES, (q + 1) * LANES)),
        r["sum0"],
    )
    z0[last_at] = gate(0, last_normed).reshape(2 * rows, block, inner)
    entering = within(0, sequence, kept, size0, r["neg0"])
    state = arrived(0, True)
    weights[2].wait()

    def second_copy(chunk, mask):
        to = xor(me, mask, bits)
        return remote(
            o1.at[at_rows(to), chunk * ocols : (chunk + 1) * ocols, :],
            r2.at[:, pl.ds(pl.multiple_of(me * block + chunk * ocols, ocols), ocols), :],
            r["s2"].at[chunk, mask],
            r["v2"].at[chunk, mask],
            to,
        )

    def own2_copy(chunk):
        return pltpu.make_async_copy(
            o1.at[at_rows(me), chunk * ocols : (chunk + 1) * ocols, :],
            r2.at[:, pl.ds(pl.multiple_of(me * block + chunk * ocols, ocols), ocols), :],
            r["l_sem"].at[1 + chunk],
        )

    def edge2_copy(j):
        return remote(
            o1.at[rows * j - 1, pl.ds(block - edge, edge), :],
            edge2,
            r["e2s"].at[j],
            r["e2r"],
            j,
        )

    edge2_own = pltpu.make_async_copy(
        o1.at[rows * (n - 1) - 1, pl.ds(block - edge, edge), :], edge2, r["l_sem"].at[1 + chunks]
    )

    for chunk in reversed(range(chunks)):
        ys = []
        for g in reversed(range(chunk * ocols // SUB, (chunk + 1) * ocols // SUB)):
            inter, state = step_out(g, entering, state)
            y = y0[g * size0 : (g + 1) * size0, :] + inter
            ys.insert(0, y.reshape(full, SUB, inner))
        at = slice(chunk * ocols, (chunk + 1) * ocols)
        flat = full * ocols
        y = jnp.concatenate(ys, axis=1).reshape(flat, inner)
        after = finish(0, y, z0[:, at, :].reshape(flat, inner), r1[:, at, :].reshape(flat, width))
        o1[:, at, :] = after.reshape(full, ocols, width)
        for mask in range(1, n):
            second_copy(chunk, mask).start()
        own2_copy(chunk).start()
        if chunk == chunks - 1:

            @pl.when(me == n - 1)
            def _():
                for j in range(1, n - 1):
                    edge2_copy(j).start()
                edge2_own.start()

    x1, z1 = r["x1"], r["z1"]
    weights[1].wait()
    pair = 2 * block
    for k in range(chips):
        source = xor(chip, k, bits - 1)
        for chunk in reversed(range(chunks)):
            if k == 0:
                own2_copy(chunk).wait()
                second_copy(chunk, 1).wait_recv()
            else:
                second_copy(chunk, 2 * k).wait_recv()
                second_copy(chunk, 2 * k + 1).wait_recv()
        at = pl.ds(pl.multiple_of(source * pair, pair), pair)
        count = rows * pair
        u = r2[:, at, :].reshape(count, width)
        if k == chips - 1:

            @pl.when((me > 0) & (me < n - 1))
            def _():
                edge2_copy(1).wait_recv()

            @pl.when(me == n - 1)
            def _():
                edge2_own.wait()

            edge_in = edge2[...]
            if edge < EDGE:
                edge_in = jnp.concatenate([jnp.zeros((EDGE - edge, width), BF16), edge_in], axis=0)
            u = jnp.concatenate([u, edge_in], axis=0)
        normed, x, p = project(1, u)

        def put(to_row, from_row):
            p1[to_row, 0:proj] = p[from_row]
            for q in range(inner // LANES):
                x1[q, to_row, :] = x[from_row, q * LANES : (q + 1) * LANES]

        for i in range(rows):
            to_row = pl.ds(pl.multiple_of(EDGE + i * cols + source * pair, SUB), pair)
            put(to_row, slice(i * pair, (i + 1) * pair))
        if k < chips - 1:
            sz = gate(1, normed)
            for i in range(rows):
                to_row = pl.ds(pl.multiple_of(i * cols + source * pair, SUB), pair)
                z1[to_row, :] = sz[i * pair : (i + 1) * pair]
        else:
            last_normed = normed[0:count]
            put(slice(0, EDGE), slice(count, count + EDGE))

    groups1 = tokens // size1

    def windows1(ref, g, lead):
        first = EDGE - (taps - 1) + g * size1
        lines = [
            ref[lead + (pl.ds(first + i, SUB, stride=lines1), slice(None))]
            for i in range(lines1 + taps - 1)
        ]
        return [jnp.concatenate(lines[k : k + lines1], axis=0) for k in range(taps)]

    sequence, kept = before(
        1,
        False,
        groups1,
        size1,
        lambda g: windows1(p1, g, ()),
        lambda g, q: windows1(x1, g, (q,)),
        r["sum1"],
    )
    sz = gate(1, last_normed)
    source = xor(chip, chips - 1, bits - 1)
    for i in range(rows):
        to_row = pl.ds(pl.multiple_of(i * cols + source * pair, SUB), pair)
        z1[to_row, :] = sz[i * pair : (i + 1) * pair]
    entering = within(1, sequence, kept, size1, r["neg1"])
    for mask in range(1, n):
        first_copy(mask).wait_send()
        for chunk in range(chunks):
            second_copy(chunk, mask).wait_send()
    for source in range(sources):

        @pl.when(me == source)
        def _():
            for j in range(n - 1):
                if j != source:
                    edge1_copy(source, j).wait_send()

    @pl.when(me == n - 1)
    def _():
        for j in range(1, n - 1):
            edge2_copy(j).wait_send()

    def states_sent(layer):
        for to in targets(layer == 0):

            @pl.when(later(me, to, layer == 0))
            def _():
                for i in range(parts):
                    state_copy(layer, i, me, to).wait_send()

    states_sent(0)
    state = arrived(1, False)
    per_row = groups1 // rows
    for i in range(rows):
        ys = []
        for g in range(i * per_row, (i + 1) * per_row):
            inter, state = step_out(g, entering, state)
            here = slice(g * size1, (g + 1) * size1)
            y = jnp.concatenate([y1[q, here, :] for q in range(inner // LANES)], axis=1)
            ys.append(y + inter)
        y = jnp.concatenate(ys, axis=0)
        out[i] = finish(1, y, z1[i * cols : (i + 1) * cols, :], r2[i])
    states_sent(1)


def on_device(n, *arrays):
    slide, in_weight, out_weight = arrays[0], arrays[2], arrays[10]
    rows, cols, width = slide.shape
    full, block, tokens = rows * n, cols // n, rows * cols
    inner = in_weight.shape[2] // 2
    edge = min(EDGE, block)
    taps = arrays[4].shape[1]
    sources = -(-(taps - 1) // rows)
    chunks = block // min(16, block)
    size0, size1 = full * SUB, min(LANES, cols)
    groups = max(tokens // size0, tokens // size1)
    parts = inner // 256
    state_weight = jnp.transpose(arrays[3], (2, 0, 1))
    operands = dict(
        slide=slide,
        norm_gain_hbm=arrays[1],
        in_hbm=in_weight,
        state_weight_hbm=state_weight,
        conv_weight_hbm=arrays[4],
        conv_bias_hbm=arrays[5],
        step_bias_hbm=arrays[6],
        decay_log_hbm=arrays[7],
        skip_gain_hbm=arrays[8],
        out_gain_hbm=arrays[9],
        out_hbm=out_weight,
    )
    dma = pltpu.SemaphoreType.DMA
    vmem = pltpu.VMEM
    scratch = dict(
        slide_v=vmem(slide.shape, BF16),
        in_w=vmem(in_weight.shape, BF16),
        out_w=vmem(out_weight.shape, BF16),
        norm_gain=vmem(arrays[1].shape, F32),
        state_weight=vmem(state_weight.shape, BF16),
        conv_weight=vmem(arrays[4].shape, F32),
        conv_bias=vmem(arrays[5].shape, F32),
        step_bias=vmem(arrays[6].shape, F32),
        decay_log=vmem(arrays[7].shape, F32),
        skip_gain=vmem(arrays[8].shape, F32),
        out_gain=vmem(arrays[9].shape, F32),
        state_w=vmem((2, state_weight.shape[0], width), BF16),
        small=vmem((2, 8, LANES), F32),
        packf=vmem((n, EDGE, LANES), F32),
        pack=vmem((n, EDGE, LANES), BF16),
        edge1=vmem((sources, EDGE, LANES), BF16),
        edge2=vmem((edge, width), BF16),
        edge_u=vmem((EDGE, width), F32),
        r1=vmem((full, block, width), BF16),
        o1=vmem((full, block, width), BF16),
        r2=vmem((rows, cols, width), BF16),
        x0=vmem((full + taps - 1, block, inner), F32),
        p0=vmem((full + taps - 1, block, LANES), F32),
        z0=vmem((full, block, inner), F32),
        x1=vmem((inner // LANES, tokens + EDGE, LANES), F32),
        p1=vmem((tokens + EDGE, LANES), F32),
        z1=vmem((tokens, inner), F32),
        xc=vmem((tokens, inner), BF16),
        y0=vmem((tokens, inner), F32),
        y1=vmem((inner // LANES, tokens, LANES), F32),
        ent1=vmem((2, tokens, LANES), F32),
        neg0=vmem((size0, size0), F32),
        neg1=vmem((size1, size1), F32),
        sum0=vmem((size0, size0), BF16),
        sum1=vmem((size1, size1), BF16),
        diag=vmem((HEADS * STATE, inner), BF16),
        local=vmem((groups, STATE, inner), F32),
        grown_last=vmem((SUB, inner), F32),
        sent=vmem((2, parts, STATE, 256 + LANES), BF16),
        gathered=vmem((2, n, parts, STATE, 256 + LANES), BF16),
        w_sem=dma((12,)),
        l_sem=dma((2 + chunks,)),
        s1=dma((n,)),
        v1=dma((n,)),
        e1s=dma((n,)),
        e1r=dma((sources,)),
        s2=dma((chunks, n)),
        v2=dma((chunks, n)),
        e2s=dma((n,)),
        e2r=dma,
        gs=dma((2, parts, n)),
        gr=dma((2, parts, n)),
    )
    names = list(operands) + ["out"] + list(scratch)
    return pl.pallas_call(
        functools.partial(kernel, n, names),
        out_shape=vmem((rows, cols, width), BF16),
        in_specs=[pl.BlockSpec(memory_space=pl.ANY)] * len(operands),
        out_specs=pl.BlockSpec(memory_space=vmem),
        scratch_shapes=list(scratch.values()),
        compiler_params=pltpu.CompilerParams(
            collective_id=0, has_side_effects=True, vmem_limit_bytes=56 * 1024 * 1024
        ),
    )(*operands.values())


def solution(mesh):
    placed = (P(("dp", "seq"), None, None),) + (P(),) * 10
    return jax.shard_map(
        functools.partial(on_device, mesh.shape["seq"]),
        mesh=mesh,
        in_specs=placed,
        out_specs=P(("dp", "seq"), None, None),
        check_vma=False,
    )
```

```python
import functools
import math

import jax
import jax.numpy as jnp
from jax import lax
from jax.experimental import pallas as pl
from jax.experimental.pallas import tpu as pltpu
from jax.sharding import PartitionSpec as P

HEADS = 12
HEADDIM = 64
STATE = 16
LANES = 128
SUB = 8
EDGE = 16
EPS = 1e-05
LOG2E = math.log2(math.e)
MESH = pl.DeviceIdType.MESH
F32 = jnp.float32
BF16 = jnp.bfloat16


def silu(v):
    half = 0.5 * v
    return half + half * jnp.tanh(half)


def rms(v, gain):
    return v * lax.rsqrt(jnp.mean(v * v, axis=-1, keepdims=True) + EPS) * gain


def iota(shape, dim):
    return lax.broadcasted_iota(jnp.int32, shape, dim)


def dot(a, b):
    return jnp.dot(a, b, preferred_element_type=F32)


def dot_nt(a, b):
    return lax.dot_general(a, b, (((1,), (1,)), ((), ())), preferred_element_type=F32)


def xor(a, b, bits):
    total = 0
    for i in range(bits):
        total = total + lax.rem(a // 2**i + b // 2**i, 2) * 2**i
    return total


def kernel(n, names, *all_refs):
    r = dict(zip(names, all_refs))
    out = r["out"]
    slide, in_hbm, out_hbm = r["slide"], r["in_hbm"], r["out_hbm"]
    me = lax.axis_index("seq")
    rows, cols, width = slide.shape
    full = rows * n
    block = cols // n
    tokens = rows * cols
    inner = in_hbm.shape[2] // 2
    taps = r["conv_weight_hbm"].shape[1]
    proj = r["state_weight_hbm"].shape[0]
    bits = n.bit_length() - 1
    chips = n // 2
    chip = me // 2
    sources = -(-(taps - 1) // rows)
    pieces = width // LANES
    edge = min(EDGE, block)
    ocols = min(16, block)
    chunks = block // ocols
    size0 = full * SUB
    size1 = min(LANES, cols)
    lines1 = size1 // SUB
    part = 256
    parts = inner // part

    def remote(src, dst, send_sem, recv_sem, to):
        return pltpu.make_async_remote_copy(
            src_ref=src,
            dst_ref=dst,
            send_sem=send_sem,
            recv_sem=recv_sem,
            device_id={"seq": to},
            device_id_type=MESH,
        )

    barrier = pltpu.get_barrier_semaphore()
    for k in range(1, n):
        pl.semaphore_signal(
            barrier, inc=1, device_id={"seq": lax.rem(me + k, n)}, device_id_type=MESH
        )

    w_sem = r["w_sem"]
    local_in = [pltpu.make_async_copy(slide, r["slide_v"], w_sem.at[0])]
    small_names = [name[:-4] for name in names if name.endswith("_hbm") and name[:-4] in names]
    small_names = [name for name in small_names if name not in ("in", "out")]
    smalls = [
        pltpu.make_async_copy(r[name + "_hbm"], r[name], w_sem.at[1 + i])
        for i, name in enumerate(small_names)
    ]
    base = 1 + len(small_names)
    weights = [
        pltpu.make_async_copy(in_hbm.at[0], r["in_w"].at[0], w_sem.at[base]),
        pltpu.make_async_copy(in_hbm.at[1], r["in_w"].at[1], w_sem.at[base + 1]),
        pltpu.make_async_copy(out_hbm, r["out_w"], w_sem.at[base + 2]),
    ]
    local_in[0].start()
    for copy in smalls:
        copy.start()
    weights[0].start()
    weights[2].start()
    weights[1].start()

    norm_gain, conv_weight, conv_bias = r["norm_gain"], r["conv_weight"], r["conv_bias"]
    in_w, out_w, out_gain = r["in_w"], r["out_w"], r["out_gain"]
    slide_v, r1, r2, o1 = r["slide_v"], r["r1"], r["r2"], r["o1"]
    edge1, edge2, pack = r["edge1"], r["edge2"], r["pack"]

    def at_cols(j):
        return pl.ds(pl.multiple_of(j * block, block), block)

    def at_rows(j):
        return pl.ds(j * rows, rows)

    local_in[0].wait()
    packf = r["packf"]
    packf[...] = jnp.zeros_like(packf)
    for j in range(n - 1):
        for i in range(rows):
            at = (j + 1) * block
            line = slide_v[i, at : at + SUB, :].astype(F32)
            for q in range(pieces):
                packf[j, i * pieces + q : i * pieces + q + 1, :] = line[
                    0:1, q * LANES : (q + 1) * LANES
                ]
    pack[...] = packf[...].astype(BF16)

    r["gathered"][...] = jnp.zeros_like(r["gathered"])
    pl.semaphore_wait(barrier, n - 1)

    def first_copy(mask):
        to = xor(me, mask, bits)
        return remote(
            slide_v.at[:, at_cols(to), :],
            r1.at[at_rows(me)],
            r["s1"].at[mask],
            r["v1"].at[mask],
            to,
        )

    for mask in range(1, n):
        first_copy(mask).start()

    def edge1_copy(source, j):
        return remote(
            pack.at[j],
            edge1.at[source],
            r["e1s"].at[j],
            r["e1r"].at[source],
            j,
        )

    for source in range(sources):

        @pl.when(me == source)
        def _():
            for j in range(n - 1):
                if j != source:
                    edge1_copy(source, j).start()
            edge1[source] = pack[source]

    own = pltpu.make_async_copy(slide_v.at[:, at_cols(me), :], r1.at[at_rows(me)], r["l_sem"].at[0])
    own.start()

    @pl.when(me == n - 1)
    def _():
        edge1[...] = jnp.zeros_like(edge1)

    @pl.when(me == 0)
    def _():
        edge2[...] = jnp.zeros_like(edge2)

    head_mask = iota((STATE, inner), 0) == iota((STATE, inner), 1) // HEADDIM

    def spread(column):
        return jnp.sum(jnp.where(head_mask, column, 0.0), axis=0, keepdims=True)

    diag = r["diag"]
    diag[...] = jnp.where(
        iota((HEADS * STATE, inner), 0) // STATE == iota((HEADS * STATE, inner), 1) // HEADDIM,
        1.0,
        0.0,
    ).astype(BF16)

    def key(v, lines):
        return lax.rem(v, SUB) * lines + v // SUB

    order0 = [key(iota((size0, size0), i), full) for i in range(2)]
    order1 = [key(iota((size1, size1), i), lines1) for i in range(2)]
    r["neg0"][...] = jnp.where(order0[1] >= order0[0], 0.0, -jnp.inf)
    r["sum0"][...] = jnp.where(order0[0] >= order0[1], 1.0, 0.0).astype(BF16)
    r["neg1"][...] = jnp.where(order1[1] <= order1[0], 0.0, -jnp.inf)
    r["sum1"][...] = jnp.where(order1[0] <= order1[1], 1.0, 0.0).astype(BF16)

    small = r["small"]
    small[...] = jnp.zeros_like(small)
    p0, p1 = r["p0"], r["p1"]
    p0[...] = jnp.zeros_like(p0)
    p1[...] = jnp.zeros_like(p1)
    edge_u = r["edge_u"]
    edge_u[...] = jnp.zeros_like(edge_u)
    for copy in smalls:
        copy.wait()
    columns = []
    for layer in range(2):
        small[layer, 0:taps, 0 : 2 * STATE] = conv_weight[layer, :, inner : inner + 2 * STATE]
        small[layer, 4:5, 0 : 2 * STATE] = conv_bias[layer : layer + 1, inner : inner + 2 * STATE]
        small[layer, 5:6, 0:HEADS] = r["step_bias"][layer : layer + 1, :]
        small[layer, 6:7, 0:HEADS] = r["decay_log"][layer : layer + 1, :]
        small[layer, 7:8, 0:HEADS] = r["skip_gain"][layer : layer + 1, :]
        r["state_w"][layer] = r["state_weight"][:, layer, :]
        turned = jnp.transpose(small[layer])
        columns.append([turned[0:STATE, 5 + i : 6 + i] for i in range(3)])

    def project(layer, u):
        normed = rms(u.astype(F32), norm_gain[layer : layer + 1, :]).astype(BF16)
        p = dot_nt(normed, r["state_w"][layer]).astype(BF16).astype(F32)
        x = dot(normed, in_w[layer, :, inner:]).astype(BF16).astype(F32)
        return normed, x, p

    def gate(layer, normed):
        return silu(dot(normed, in_w[layer, :, :inner]).astype(BF16).astype(F32))

    xc_ref, y0, y1, ent1 = r["xc"], r["y0"], r["y1"], r["ent1"]

    def state_copy(layer, i, source, to):
        wide = part + LANES if i == 0 else part
        return remote(
            r["sent"].at[layer, i, :, 0:wide],
            r["gathered"].at[layer, source, i, :, 0:wide],
            r["gs"].at[layer, i, to],
            r["gr"].at[layer, i, source],
            to,
        )

    def targets(backward):
        return range(0, n - 1) if backward else range(n - 1, 0, -1)

    def later(i, j, backward):
        return (i > j) if backward else (i < j)

    def before(layer, backward, groups, size, load_p, load_x, sum_ref):
        bias, decay_col, _ = columns[layer]
        rate_scale = -jnp.exp(decay_col) * LOG2E
        last_at = 0 if backward else size - 1
        sequence = list(range(groups))[:: -1 if backward else 1]
        turned, c_side = {}, {}
        lane = iota((size, LANES), 1)
        for g in sequence:
            windows = load_p(g)
            total = small[layer, 4:5, :] + small[layer, 0:1, :] * windows[0]
            for k in range(1, taps):
                total = total + small[layer, k : k + 1, :] * windows[k]
            bc = silu(total).astype(BF16).astype(F32)
            turned[g] = jnp.transpose(jnp.where(lane < 2 * STATE, bc, windows[-1]))
            c_side[g] = jnp.where((lane >= STATE) & (lane < 2 * STATE), bc, 0.0).astype(BF16)
        raw = bias + jnp.concatenate(
            [turned[g][2 * STATE : 3 * STATE] for g in sequence], axis=1
        )
        step = jnp.maximum(raw, 0.0) + jnp.log1p(jnp.exp(-jnp.abs(raw)))
        rate = step * rate_scale
        high = rate.astype(BF16)
        low = (rate - high.astype(F32)).astype(BF16)
        split = jnp.concatenate([high, low], axis=0)
        log_step = jnp.log2(step)
        total_last, kept, weighted, grown_last = None, {}, {}, {}
        for i, g in enumerate(sequence):
            at = slice(i * size, (i + 1) * size)
            both = dot(split[:, at], sum_ref[...])
            cum = both[0:STATE] + both[STATE : 2 * STATE]
            less = cum - log_step[:, at]
            last = cum[:, last_at : last_at + 1]
            tail = jnp.exp2(last - less)
            b_rows = turned[g][0:STATE]
            weighted[g] = jnp.concatenate(
                [b_rows * tail[h : h + 1, :] for h in range(HEADS)], axis=0
            ).astype(BF16)
            grown_last[g] = spread(jnp.exp2(last))
            r["grown_last"][g : g + 1, :] = grown_last[g]
            total_last = last if total_last is None else total_last + last
            kept[g] = (turned[g], c_side[g], cum, less)
        decay = jnp.exp2(total_last)
        decay_high = decay.astype(BF16).astype(F32)
        lane = iota((STATE, LANES), 1)
        sent = r["sent"]
        sent[layer, 0, :, part : part + LANES] = jnp.where(
            lane == 0, decay_high, jnp.where(lane == 1, decay - decay_high, 0.0)
        ).astype(BF16)
        heads_per = part // HEADDIM
        lane = iota((STATE, part), 1) // HEADDIM
        for i in range(parts):
            whole = slice(i * part, (i + 1) * part)
            carried = None
            for g in sequence:
                here = slice(g * size, (g + 1) * size)
                for q in range(i * part // LANES, (i + 1) * part // LANES):
                    at = slice(q * LANES, (q + 1) * LANES)
                    windows = load_x(g, q)
                    low = [w.astype(BF16) for w in windows]
                    total = conv_bias[layer : layer + 1, at].astype(BF16) + (
                        conv_weight[layer, 0:1, at].astype(BF16) * low[0]
                    )
                    for k in range(1, taps):
                        total = total + conv_weight[layer, k : k + 1, at].astype(BF16) * low[k]
                    xc_ref[here, at] = silu(total)
                got = dot(
                    weighted[g][i * heads_per * STATE : (i + 1) * heads_per * STATE],
                    xc_ref[here, whole],
                )
                local = got[0:STATE]
                for h in range(1, heads_per):
                    local = jnp.where(lane == h, got[h * STATE : (h + 1) * STATE], local)
                r["local"][g, :, whole] = local
                carried = local if carried is None else grown_last[g][:, whole] * carried + local
            sent[layer, i, :, 0:part] = carried.astype(BF16)
            for to in targets(backward):

                @pl.when(later(me, to, backward))
                def _():
                    state_copy(layer, i, me, to).start()

        return sequence, kept

    def within(layer, sequence, kept, size, neg_ref):
        skip = spread(columns[layer][2])
        even = iota((size, LANES), 1) < HEADDIM
        entering = {}
        for g in sequence:
            here = slice(g * size, (g + 1) * size)
            turned, c_side, cum, less = kept[g]
            b_rows, c_rows = turned[0:STATE], turned[STATE : 2 * STATE]
            both_b = [b_rows, b_rows, jnp.zeros((LANES - 2 * STATE, size), F32)]
            scores = dot(c_side, jnp.concatenate(both_b, axis=0).astype(BF16))
            grown = jnp.exp2(cum)
            stack = [c_rows * grown[h : h + 1, :] for h in range(HEADS)] + [cum]
            stack.append(jnp.zeros((-STATE * (HEADS + 1) % LANES, size), F32))
            across = jnp.transpose(jnp.concatenate(stack, axis=0))
            if layer == 0:
                entering[g] = across[:, 0 : HEADS * STATE].astype(BF16)
            else:
                for q in range(2):
                    for i in range(lines1):
                        ent1[q, pl.ds(g * size + i, SUB, stride=lines1), :] = across[
                            i * SUB : (i + 1) * SUB, q * LANES : (q + 1) * LANES
                        ]
            for pair in range(HEADS // 2):
                at = slice(pair * LANES, (pair + 1) * LANES)
                xp = xc_ref[here, at]
                weights = []
                for h in (2 * pair, 2 * pair + 1):
                    column = across[:, HEADS * STATE + h : HEADS * STATE + h + 1]
                    diff = (column - less[h : h + 1, :]) + neg_ref[...]
                    weights.append((scores * jnp.exp2(diff)).astype(BF16))
                zero = jnp.zeros_like(xp)
                stacked = jnp.concatenate(
                    [jnp.where(even, xp, zero), jnp.where(even, zero, xp)], axis=0
                )
                y = skip[:, at] * xp.astype(F32) + dot(jnp.concatenate(weights, axis=1), stacked)
                if layer == 0:
                    y0[here, at] = y
                else:
                    for i in range(lines1):
                        y1[pair, pl.ds(g * size + i, SUB, stride=lines1), :] = y[
                            i * SUB : (i + 1) * SUB
                        ]
        if layer == 1:
            for g in sequence:
                here = slice(g * size, (g + 1) * size)
                entering[g] = jnp.concatenate(
                    [ent1[0, here, :], ent1[1, here, 0 : HEADS * STATE - LANES]], axis=1
                ).astype(BF16)
        return entering

    def arrived(layer, backward, sequence, enter):
        gathered = r["gathered"]
        factors, waiting = {}, []
        order = range(n - 1, 0, -1) if backward else range(0, n - 1)
        for i in range(parts):
            whole = slice(i * part, (i + 1) * part)
            for source in order:

                @pl.when(later(source, me, backward))
                def _():
                    state_copy(layer, i, source, (source + 1) % n).wait_recv()

            total = jnp.zeros((STATE, part), F32)
            for source in order:
                valid = later(source, me, backward)
                if i == 0:
                    packed = gathered[layer, source, 0, :, part : part + LANES].astype(F32)
                    factor = spread(jnp.sum(packed, axis=1, keepdims=True))
                    factors[source] = jnp.where(valid, factor, 1.0)
                came = gathered[layer, source, i, :, 0:part].astype(F32)
                total = factors[source][:, whole] * total + jnp.where(valid, came, 0.0)
            if layer == 1:
                waiting.append(total)
            elif i < parts - 1:
                for g in sequence:
                    total = enter(g, i, total)
        for i, total in enumerate(waiting[:-1]):
            for g in sequence:
                total = enter(g, i, total)
        return waiting[-1] if waiting else total

    def next_state(g, i, entering, state):
        whole = slice(i * part, (i + 1) * part)
        low = state.astype(BF16)
        wide = jnp.concatenate([low] * HEADS, axis=0) * diag[:, whole]
        inter = dot(entering[g], wide)
        return inter, r["grown_last"][g : g + 1, whole] * state + r["local"][g, :, whole]

    def finish(layer, gated, token):
        scale = lax.rsqrt(jnp.mean(gated * gated, axis=-1, keepdims=True) + EPS)
        mixed = (gated * out_gain[layer : layer + 1, :]).astype(BF16)
        return (token.astype(F32) + scale * dot(mixed, out_w[layer])).astype(BF16)

    x0, z0 = r["x0"], r["z0"]
    weights[0].wait()
    last_normed = None
    for k in range(chips):
        source = xor(chip, k, bits - 1)
        if k == 0:
            own.wait()
            first_copy(1).wait_recv()
        else:
            first_copy(2 * k).wait_recv()
            first_copy(2 * k + 1).wait_recv()
        if k == chips - 1:
            for i in range(sources):

                @pl.when((me != i) & (me < n - 1))
                def _():
                    edge1_copy(i, 0 if i else 1).wait_recv()

            for i in range(taps - 1):
                line = edge1[i // rows].astype(F32)
                for q in range(pieces):
                    j = (i % rows) * pieces + q
                    edge_u[i : i + 1, q * LANES : (q + 1) * LANES] = line[j : j + 1, :]
        at = pl.ds(source * 2 * rows, 2 * rows)
        count = 2 * rows * block
        u = r1[at].reshape(count, width)
        if k == chips - 1:
            u = jnp.concatenate([u, edge_u[...].astype(BF16)], axis=0)
        normed, x, p = project(0, u)
        p0[at, :, 0:proj] = p[0:count].reshape(2 * rows, block, proj)
        x0[at] = x[0:count].reshape(2 * rows, block, inner)
        if k < chips - 1:
            z0[at] = gate(0, normed).reshape(2 * rows, block, inner)
        else:
            last_normed, last_at = normed[0:count], at
            edge_x = x[count:]
            edge_p = jnp.concatenate(
                [p[count:], jnp.zeros((EDGE, LANES - proj), F32)], axis=1
            )
    for i in range(taps - 1):
        for ref, line in ((p0, edge_p), (x0, edge_x)):
            wide = ref.shape[2]
            moved = pltpu.roll(ref[i], block - 1, 0)
            final = iota((block, wide), 0) == block - 1
            ref[full + i] = jnp.where(final, line[i : i + 1, :], moved)

    groups0 = block // SUB

    def windows0(ref, g, at):
        first = [taps - 1 - k for k in range(taps)]
        at_g = slice(g * SUB, (g + 1) * SUB)
        return [ref[i : i + full, at_g, at].reshape(size0, LANES) for i in first]

    sequence, kept = before(
        0,
        True,
        groups0,
        size0,
        lambda g: windows0(p0, g, slice(0, LANES)),
        lambda g, q: windows0(x0, g, slice(q * LANES, (q + 1) * LANES)),
        r["sum0"],
    )
    z0[last_at] = gate(0, last_normed).reshape(2 * rows, block, inner)
    entering = within(0, sequence, kept, size0, r["neg0"])

    def enter0(g, i, state):
        inter, state = next_state(g, i, entering, state)
        here, whole = slice(g * size0, (g + 1) * size0), slice(i * part, (i + 1) * part)
        sz = z0[:, g * SUB : (g + 1) * SUB, whole].reshape(size0, part)
        y0[here, whole] = (y0[here, whole] + inter) * sz
        return state

    state = arrived(0, True, sequence, enter0)
    weights[2].wait()

    def second_copy(chunk, mask):
        to = xor(me, mask, bits)
        return remote(
            o1.at[at_rows(to), chunk * ocols : (chunk + 1) * ocols, :],
            r2.at[:, pl.ds(pl.multiple_of(me * block + chunk * ocols, ocols), ocols), :],
            r["s2"].at[chunk, mask],
            r["v2"].at[chunk, mask],
            to,
        )

    def own2_copy(chunk):
        return pltpu.make_async_copy(
            o1.at[at_rows(me), chunk * ocols : (chunk + 1) * ocols, :],
            r2.at[:, pl.ds(pl.multiple_of(me * block + chunk * ocols, ocols), ocols), :],
            r["l_sem"].at[1 + chunk],
        )

    def edge2_copy(j):
        return remote(
            o1.at[rows * j - 1, pl.ds(block - edge, edge), :],
            edge2,
            r["e2s"].at[j],
            r["e2r"],
            j,
        )

    edge2_own = pltpu.make_async_copy(
        o1.at[rows * (n - 1) - 1, pl.ds(block - edge, edge), :], edge2, r["l_sem"].at[1 + chunks]
    )

    for chunk in reversed(range(chunks)):
        ys = []
        for g in reversed(range(chunk * ocols // SUB, (chunk + 1) * ocols // SUB)):
            state = enter0(g, parts - 1, state)
            y = y0[g * size0 : (g + 1) * size0, :]
            ys.insert(0, y.reshape(full, SUB, inner))
        at = slice(chunk * ocols, (chunk + 1) * ocols)
        flat = full * ocols
        y = jnp.concatenate(ys, axis=1).reshape(flat, inner)
        after = finish(0, y, r1[:, at, :].reshape(flat, width))
        o1[:, at, :] = after.reshape(full, ocols, width)
        for mask in range(1, n):
            second_copy(chunk, mask).start()
        own2_copy(chunk).start()
        if chunk == chunks - 1:

            @pl.when(me == n - 1)
            def _():
                for j in range(1, n - 1):
                    edge2_copy(j).start()
                edge2_own.start()

    x1, z1 = r["x1"], r["z1"]
    weights[1].wait()
    pair = 2 * block
    for k in range(chips):
        source = xor(chip, k, bits - 1)
        for chunk in reversed(range(chunks)):
            if k == 0:
                own2_copy(chunk).wait()
                second_copy(chunk, 1).wait_recv()
            else:
                second_copy(chunk, 2 * k).wait_recv()
                second_copy(chunk, 2 * k + 1).wait_recv()
        at = pl.ds(pl.multiple_of(source * pair, pair), pair)
        count = rows * pair
        u = r2[:, at, :].reshape(count, width)
        if k == chips - 1:

            @pl.when((me > 0) & (me < n - 1))
            def _():
                edge2_copy(1).wait_recv()

            @pl.when(me == n - 1)
            def _():
                edge2_own.wait()

            edge_in = edge2[...]
            if edge < EDGE:
                edge_in = jnp.concatenate([jnp.zeros((EDGE - edge, width), BF16), edge_in], axis=0)
            u = jnp.concatenate([u, edge_in], axis=0)
        normed, x, p = project(1, u)

        def put(to_row, from_row):
            p1[to_row, 0:proj] = p[from_row]
            for q in range(inner // LANES):
                x1[q, to_row, :] = x[from_row, q * LANES : (q + 1) * LANES]

        for i in range(rows):
            to_row = pl.ds(pl.multiple_of(EDGE + i * cols + source * pair, SUB), pair)
            put(to_row, slice(i * pair, (i + 1) * pair))
        if k < chips - 1:
            sz = gate(1, normed)
            for i in range(rows):
                to_row = pl.ds(pl.multiple_of(i * cols + source * pair, SUB), pair)
                z1[to_row, :] = sz[i * pair : (i + 1) * pair]
        else:
            last_normed = normed[0:count]
            put(slice(0, EDGE), slice(count, count + EDGE))

    groups1 = tokens // size1

    def windows1(ref, g, lead):
        first = EDGE - (taps - 1) + g * size1
        lines = [
            ref[lead + (pl.ds(first + i, SUB, stride=lines1), slice(None))]
            for i in range(lines1 + taps - 1)
        ]
        return [jnp.concatenate(lines[k : k + lines1], axis=0) for k in range(taps)]

    sequence, kept = before(
        1,
        False,
        groups1,
        size1,
        lambda g: windows1(p1, g, ()),
        lambda g, q: windows1(x1, g, (q,)),
        r["sum1"],
    )
    sz = gate(1, last_normed)
    source = xor(chip, chips - 1, bits - 1)
    for i in range(rows):
        to_row = pl.ds(pl.multiple_of(i * cols + source * pair, SUB), pair)
        z1[to_row, :] = sz[i * pair : (i + 1) * pair]
    entering = within(1, sequence, kept, size1, r["neg1"])
    for mask in range(1, n):
        first_copy(mask).wait_send()
        for chunk in range(chunks):
            second_copy(chunk, mask).wait_send()
    for source in range(sources):

        @pl.when(me == source)
        def _():
            for j in range(n - 1):
                if j != source:
                    edge1_copy(source, j).wait_send()

    @pl.when(me == n - 1)
    def _():
        for j in range(1, n - 1):
            edge2_copy(j).wait_send()

    def states_sent(layer):
        for to in targets(layer == 0):

            @pl.when(later(me, to, layer == 0))
            def _():
                for i in range(parts):
                    state_copy(layer, i, me, to).wait_send()

    states_sent(0)

    def enter1(g, i, state):
        inter, state = next_state(g, i, entering, state)
        here = slice(g * size1, (g + 1) * size1)
        for q in range(part // LANES):
            at = i * part // LANES + q
            y1[at, here, :] = (y1[at, here, :] + inter[:, q * LANES : (q + 1) * LANES]) * z1[
                here, at * LANES : (at + 1) * LANES
            ]
        return state

    state = arrived(1, False, sequence, enter1)
    per_row = groups1 // rows
    for i in range(rows):
        ys = []
        for g in range(i * per_row, (i + 1) * per_row):
            state = enter1(g, parts - 1, state)
            here = slice(g * size1, (g + 1) * size1)
            y = jnp.concatenate([y1[q, here, :] for q in range(inner // LANES)], axis=1)
            ys.append(y)
        y = jnp.concatenate(ys, axis=0)
        out[i] = finish(1, y, r2[i])
    states_sent(1)


def on_device(n, *arrays):
    slide, in_weight, out_weight = arrays[0], arrays[2], arrays[10]
    rows, cols, width = slide.shape
    full, block, tokens = rows * n, cols // n, rows * cols
    inner = in_weight.shape[2] // 2
    edge = min(EDGE, block)
    taps = arrays[4].shape[1]
    sources = -(-(taps - 1) // rows)
    chunks = block // min(16, block)
    size0, size1 = full * SUB, min(LANES, cols)
    groups = max(tokens // size0, tokens // size1)
    parts = inner // 256
    state_weight = jnp.transpose(arrays[3], (2, 0, 1))
    operands = dict(
        slide=slide,
        norm_gain_hbm=arrays[1],
        in_hbm=in_weight,
        state_weight_hbm=state_weight,
        conv_weight_hbm=arrays[4],
        conv_bias_hbm=arrays[5],
        step_bias_hbm=arrays[6],
        decay_log_hbm=arrays[7],
        skip_gain_hbm=arrays[8],
        out_gain_hbm=arrays[9],
        out_hbm=out_weight,
    )
    dma = pltpu.SemaphoreType.DMA
    vmem = pltpu.VMEM
    scratch = dict(
        slide_v=vmem(slide.shape, BF16),
        in_w=vmem(in_weight.shape, BF16),
        out_w=vmem(out_weight.shape, BF16),
        norm_gain=vmem(arrays[1].shape, F32),
        state_weight=vmem(state_weight.shape, BF16),
        conv_weight=vmem(arrays[4].shape, F32),
        conv_bias=vmem(arrays[5].shape, F32),
        step_bias=vmem(arrays[6].shape, F32),
        decay_log=vmem(arrays[7].shape, F32),
        skip_gain=vmem(arrays[8].shape, F32),
        out_gain=vmem(arrays[9].shape, F32),
        state_w=vmem((2, state_weight.shape[0], width), BF16),
        small=vmem((2, 8, LANES), F32),
        packf=vmem((n, EDGE, LANES), F32),
        pack=vmem((n, EDGE, LANES), BF16),
        edge1=vmem((sources, EDGE, LANES), BF16),
        edge2=vmem((edge, width), BF16),
        edge_u=vmem((EDGE, width), F32),
        r1=vmem((full, block, width), BF16),
        o1=vmem((full, block, width), BF16),
        r2=vmem((rows, cols, width), BF16),
        x0=vmem((full + taps - 1, block, inner), F32),
        p0=vmem((full + taps - 1, block, LANES), F32),
        z0=vmem((full, block, inner), F32),
        x1=vmem((inner // LANES, tokens + EDGE, LANES), F32),
        p1=vmem((tokens + EDGE, LANES), F32),
        z1=vmem((tokens, inner), F32),
        xc=vmem((tokens, inner), BF16),
        y0=vmem((tokens, inner), F32),
        y1=vmem((inner // LANES, tokens, LANES), F32),
        ent1=vmem((2, tokens, LANES), F32),
        neg0=vmem((size0, size0), F32),
        neg1=vmem((size1, size1), F32),
        sum0=vmem((size0, size0), BF16),
        sum1=vmem((size1, size1), BF16),
        diag=vmem((HEADS * STATE, inner), BF16),
        local=vmem((groups, STATE, inner), F32),
        grown_last=vmem((SUB, inner), F32),
        sent=vmem((2, parts, STATE, 256 + LANES), BF16),
        gathered=vmem((2, n, parts, STATE, 256 + LANES), BF16),
        w_sem=dma((12,)),
        l_sem=dma((2 + chunks,)),
        s1=dma((n,)),
        v1=dma((n,)),
        e1s=dma((n,)),
        e1r=dma((sources,)),
        s2=dma((chunks, n)),
        v2=dma((chunks, n)),
        e2s=dma((n,)),
        e2r=dma,
        gs=dma((2, parts, n)),
        gr=dma((2, parts, n)),
    )
    names = list(operands) + ["out"] + list(scratch)
    return pl.pallas_call(
        functools.partial(kernel, n, names),
        out_shape=vmem((rows, cols, width), BF16),
        in_specs=[pl.BlockSpec(memory_space=pl.ANY)] * len(operands),
        out_specs=pl.BlockSpec(memory_space=vmem),
        scratch_shapes=list(scratch.values()),
        compiler_params=pltpu.CompilerParams(
            collective_id=0, has_side_effects=True, vmem_limit_bytes=56 * 1024 * 1024
        ),
    )(*operands.values())


def solution(mesh):
    placed = (P(("dp", "seq"), None, None),) + (P(),) * 10
    return jax.shard_map(
        functools.partial(on_device, mesh.shape["seq"]),
        mesh=mesh,
        in_specs=placed,
        out_specs=P(("dp", "seq"), None, None),
        check_vma=False,
    )
```
